256 devices in a mesh: facet: 128 (over x, z, y), half: 2 (over core).
Axes of the slice: x: 4, y: 4, z: 8, core: 2. Of those that a mesh axis runs over, the one named last changes fastest.
Arguments:
- facet_image: bfloat16 [128, 2048, 2048], P('facet', 'half'), may hold values from -6 to 6
- coverage: int32 [128, 8], P('facet'), may hold values 0 or 1
- row_offsets: int32 [8], replicated, may hold values from 0 to 131071
- column_offset: int32 [1], replicated, may hold values from 0 to 131071
- piece_owner: int32 [2, 128], replicated, may hold values from 0 to 127, as said below
Outputs:
- subgrid_slots: float32 [2, 128, 3, 2, 16, 512], P('half', 'facet')
The draws below stay inside these ranges and needn't reach their ends.
Inputs may be any that keep to these rules, and one draw needn't show every extreme that they name: `piece_owner`: for each half, every owner index names at most 3 of the 128 pieces, and some owner names exactly 3.
All inputs are finite; a program needn't handle non-finite values. No bound on the sum of `coverage` on one device may be relied on, other than what follows from the above.
Results may differ from the reference program's by a relative error of at most 0.0077.
Values may be sent and summed in bfloat16 or wider, within the bound.
No kernel may reach another device: no remote copies, remote signals or barrier semaphores. Data moves between devices by JAX's collectives and lax.ppermute only.
A program may use at most 64 MiB of HBM per device.

```python
import math
import jax
import jax.numpy as jnp
from jax import lax

FS = 2048
M = 256
SG = 512
IMAGE = 131072
SUBGRIDS = 8
CAP = 3
HALVES = 2
FACETS = 128
N_FACET = 128
N_HALF = 2


def draw_piece_owner(key, part):
    patterns = jnp.array([[0, 0, 0, 1], [0, 0, 1, 2], [0, 0, 1, 1]], jnp.int32)
    rows_out = []
    for half_n in range(HALVES):
        half_key = jax.random.fold_in(key, 101 + half_n)
        key_a, key_b, key_c = jax.random.split(half_key, 3)
        blocks_n = FACETS // 4
        chosen = jax.random.randint(key_a, (blocks_n,), 0, 3)
        chosen = chosen.at[0].set(0)
        local_ids = patterns[chosen]
        slot_ids = (3 * jnp.arange(blocks_n, dtype=jnp.int32)[:, None] + local_ids).reshape(FACETS)
        people = jax.random.permutation(key_b, FACETS).astype(jnp.int32)
        owners = people[slot_ids]
        order = jax.random.permutation(key_c, FACETS).astype(jnp.int32)
        rows_out.append(owners[order])
    return jnp.stack(rows_out, axis=0).astype(jnp.int32)


def place_ends(drawn, rng, low, high):
    extent = drawn.shape
    index_at = [jax.random.randint(jax.random.fold_in(rng, axis), (), 0, extent[axis]) for axis in range(len(extent))]
    drawn = drawn.at[tuple(index_at)].set(low)
    longest = extent.index(max(extent))
    index_at[longest] = (index_at[longest] + 1) % extent[longest]
    return drawn.at[tuple(index_at)].set(high)


def block_levels(stream_key, dims, cuts, least, top_value):
    def one(position, parts):
        heights = jax.random.uniform(jax.random.fold_in(jax.random.fold_in(stream_key, 6), position), (parts,), jnp.float32, least / len(cuts), top_value / len(cuts))
        return jnp.repeat(jnp.exp(heights), dims[position] // parts).reshape((-1,) + (1,) * (len(dims) - position - 1))

    factor_of = one(*cuts[0])
    for cut in cuts[1:]:
        factor_of = factor_of * one(*cut)
    return factor_of


def scatter_about(key, dims, spread, bound, cuts=(), kind=jnp.bfloat16):
    result = spread * jax.random.normal(key, dims, jnp.float32)
    if cuts:
        result = result * block_levels(key, dims, cuts, -0.22, 0.18)
    return jnp.clip(result, -bound, bound).astype(kind)


def setup_inputs(seed: int = 0) -> dict:
    keys = jax.random.split(jax.random.key(seed), 6)
    return {
        "facet_image": scatter_about(keys[0], (FACETS, FS, FS), 1.0, 6.0, ((0, 128), (1, 2))),
        "coverage": place_ends((jax.random.randint(keys[1], (FACETS, SUBGRIDS), 0, 4) < 3).astype(jnp.int32), jax.random.fold_in(keys[1], 1), 0, 1),
        "row_offsets": place_ends(jax.random.randint(keys[2], (SUBGRIDS,), 0, IMAGE), jax.random.fold_in(keys[2], 1), 0, IMAGE - 1).astype(jnp.int32),
        "column_offset": jax.random.randint(keys[3], (1,), 0, IMAGE).astype(jnp.int32),
        "piece_owner": draw_piece_owner(jax.random.fold_in(keys[5], 71), 0),
    }


TWO_PI = 2.0 * math.pi

def window_table(positions, offset, samples):
    stride = IMAGE // FS
    ticks = (jnp.arange(samples, dtype=jnp.int32) - samples // 2) * stride
    shifted = jnp.mod(offset + ticks, IMAGE)
    product = jnp.mod(positions[:, None] * shifted[None, :], IMAGE)
    phases = -TWO_PI / IMAGE * product.astype(jnp.float32)
    relative = positions.astype(jnp.float32) * (2.0 / FS)
    taper = jnp.exp(-2.0 * relative * relative) / math.sqrt(FS)
    return (taper[:, None] * jnp.cos(phases), taper[:, None] * jnp.sin(phases))

def facet_shift(facet_id):
    ratio = IMAGE // FS
    shift_a = jnp.mod(7 * facet_id, ratio) - ratio // 2
    shift_b = jnp.mod(5 * (facet_id // ratio) + 3 * facet_id, ratio) - ratio // 2
    return (shift_a, shift_b)

def long_phase(shift, offset, samples):
    stride = IMAGE // FS
    ticks = (jnp.arange(samples, dtype=jnp.int32) - samples // 2) * stride
    wrapped = jnp.mod(offset + ticks, IMAGE)
    scaled = jnp.mod(FS * wrapped, IMAGE)
    product = jnp.mod(shift * scaled, IMAGE)
    phases = -TWO_PI / IMAGE * product.astype(jnp.float32)
    return (jnp.cos(phases), jnp.sin(phases))

def grid_table():
    ticks_in = jnp.arange(M, dtype=jnp.int32) - M // 2
    ticks_out = jnp.arange(SG, dtype=jnp.int32) - SG // 2
    product = jnp.mod(ticks_in[:, None] * ticks_out[None, :], SG)
    phases = TWO_PI / SG * product.astype(jnp.float32)
    return (jnp.cos(phases) / math.sqrt(M), jnp.sin(phases) / math.sqrt(M))

def weighted_parts(part_re, part_im, cover, offsets, column, facet_id):
    shift_a, shift_b = facet_shift(facet_id)
    rot_re, rot_im = long_phase(shift_a, offsets[:, None], M)
    scaled_re = cover[:, None, None] * (rot_re[:, :, None] * part_re - rot_im[:, :, None] * part_im)
    scaled_im = cover[:, None, None] * (rot_re[:, :, None] * part_im + rot_im[:, :, None] * part_re)
    col_re, col_im = long_phase(shift_b, column, M)
    grid_re, grid_im = grid_table()
    tilt_re = col_re[:, None] * grid_re - col_im[:, None] * grid_im
    tilt_im = col_re[:, None] * grid_im + col_im[:, None] * grid_re
    return (scaled_re.astype(jnp.bfloat16), scaled_im.astype(jnp.bfloat16), tilt_re.astype(jnp.bfloat16), tilt_im.astype(jnp.bfloat16))

def to_subgrid(summed, out_table):
    item_count = summed.shape[0]
    width_cols = summed.shape[2]
    real_part = jnp.dot(summed[:, 0].reshape(item_count * width_cols, M), out_table, preferred_element_type=jnp.float32)
    imag_part = jnp.dot(summed[:, 1].reshape(item_count * width_cols, M), out_table, preferred_element_type=jnp.float32)
    out_re = (real_part[:, :SG] - imag_part[:, SG:]).reshape(item_count, width_cols, SG)
    out_im = (real_part[:, SG:] + imag_part[:, :SG]).reshape(item_count, width_cols, SG)
    return jnp.stack([out_re, out_im], axis=1)

def slot_index(owners):
    positions = jnp.arange(owners.shape[0], dtype=jnp.int32)
    same_owner = owners[:, None] == owners[None, :]
    earlier = positions[:, None] > positions[None, :]
    return lax.optimization_barrier(jnp.sum((same_owner & earlier).astype(jnp.int32), axis=1)).astype(jnp.int32)

def slot_source(owners, slot_of, targets):
    positions = jnp.arange(owners.shape[0], dtype=jnp.int32)
    levels = jnp.arange(CAP, dtype=jnp.int32)
    matches = (owners[None, None, :] == targets[:, None, None]) & (slot_of[None, None, :] == levels[None, :, None])
    source = lax.optimization_barrier(jnp.sum(jnp.where(matches, positions[None, None, :], 0), axis=2)).astype(jnp.int32)
    filled = jnp.any(matches, axis=2)
    return (source, filled)

def reference(facet_image, coverage, row_offsets, column_offset, piece_owner):
    col_place = jnp.arange(FS, dtype=jnp.int32) - FS // 2
    col_re, col_im = window_table(col_place, column_offset[0], M)
    col_table = jnp.concatenate([col_re, col_im], axis=1).astype(jnp.bfloat16)

    def row_one(offset_one):
        table_re, table_im = window_table(col_place, offset_one, M)
        return jnp.concatenate([table_re, table_im], axis=1)
    row_table = jax.vmap(row_one)(row_offsets).astype(jnp.bfloat16)
    grid_re, grid_im = grid_table()
    out_table = jnp.concatenate([grid_re, grid_im], axis=1).astype(jnp.bfloat16)
    width_cols = SG * (SUBGRIDS // N_HALF) // N_FACET
    blocks_per = SG // width_cols

    def one_facet(running, inputs):
        pixels, cover_row, facet_id = inputs
        folded = jnp.dot(pixels, col_table, preferred_element_type=jnp.float32).astype(jnp.bfloat16)
        blocks = jnp.einsum('sra,rb->sab', row_table.astype(jnp.float32), folded.astype(jnp.float32))
        part_re = blocks[:, :M, :M] - blocks[:, M:, M:]
        part_im = blocks[:, :M, M:] + blocks[:, M:, :M]
        y_re, y_im, tilt_re, tilt_im = weighted_parts(part_re, part_im, cover_row, row_offsets, column_offset[0], facet_id)
        tilt_re = tilt_re.astype(jnp.float32).reshape(M, blocks_per, width_cols)
        tilt_im = tilt_im.astype(jnp.float32).reshape(M, blocks_per, width_cols)
        y_re = y_re.astype(jnp.float32)
        y_im = y_im.astype(jnp.float32)
        piece_re = jnp.einsum('lbj,skl->sbjk', tilt_re, y_re) - jnp.einsum('lbj,skl->sbjk', tilt_im, y_im)
        piece_im = jnp.einsum('lbj,skl->sbjk', tilt_re, y_im) + jnp.einsum('lbj,skl->sbjk', tilt_im, y_re)
        pieces = jnp.stack([piece_re, piece_im], axis=2).astype(jnp.bfloat16)
        return (running + pieces.astype(jnp.float32), None)
    start = jnp.zeros((SUBGRIDS, blocks_per, 2, width_cols, M), jnp.float32)
    facet_ids = jnp.arange(N_FACET, dtype=jnp.int32)
    running, unused = lax.scan(one_facet, start, (facet_image, coverage.astype(jnp.float32), facet_ids))
    summed = (running * (1.0 / math.sqrt(N_FACET))).astype(jnp.bfloat16)
    summed = summed.reshape(N_HALF, N_FACET, 2, width_cols, M)
    outputs = []
    for half_n in range(N_HALF):
        owners = piece_owner[half_n]
        source, filled = slot_source(owners, slot_index(owners), facet_ids)
        results = to_subgrid(summed[half_n], out_table)
        outputs.append(jnp.where(filled[:, :, None, None, None], results[source], jnp.float32(0.0)))
    return jnp.stack(outputs, axis=0)
```

```python
import math

import jax
import jax.numpy as jnp
from jax import lax
from jax.sharding import PartitionSpec as P

FS = 2048
M = 256
SG = 512
IMAGE = 131072
SUBGRIDS = 8
CAP = 3
NX, NZ, NY = 4, 8, 4
GROUP = NX * NY
KB = M // GROUP
FINE = 16

TWO_PI = 2.0 * math.pi
STRIDE = IMAGE // FS


def unit(product, period, sign=-1.0):
    phases = (sign * TWO_PI / period) * jnp.mod(product, period).astype(jnp.float32)
    return jnp.cos(phases), jnp.sin(phases)


def cmul(a, b):
    return a[0] * b[0] - a[1] * b[1], a[0] * b[1] + a[1] * b[0]


def taper_of(place):
    relative = place.astype(jnp.float32) * (2.0 / FS)
    return jnp.exp(-2.0 * relative * relative) / math.sqrt(FS)


def fourier(coarse, samples=M):
    ticks = jnp.arange(samples, dtype=jnp.int32) - samples // 2
    big = unit(coarse[:, None] * ticks[None, :], FS)
    fine = jnp.arange(FINE, dtype=jnp.int32)
    small = unit(fine[:, None] * ticks[None, :], FS)
    return cmul(
        (big[0][:, None, :], big[1][:, None, :]), (small[0][None], small[1][None])
    )


def window(coarse, offsets):
    fine = jnp.arange(FINE, dtype=jnp.int32)
    place = coarse[:, None] + fine[None, :]
    taper = taper_of(place)
    turn = unit(place[None] * offsets[:, None, None], IMAGE)
    gain = (taper * turn[0])[..., None], (taper * turn[1])[..., None]
    base = fourier(coarse)
    table = cmul(gain, (base[0][None], base[1][None]))
    rows = coarse.shape[0] * FINE
    return [t.reshape(offsets.shape[0], rows, M).astype(jnp.bfloat16) for t in table]


def grid_table():
    ticks_in = jnp.arange(M, dtype=jnp.int32) - M // 2
    ticks_out = jnp.arange(SG, dtype=jnp.int32) - SG // 2
    grid = unit(ticks_in[:, None] * ticks_out[None, :], SG, 1.0)
    return [(g / math.sqrt(M)).astype(jnp.bfloat16) for g in grid]


def facet_weight(facet_id, offsets, column, cover):
    ratio = STRIDE
    shift_a = jnp.mod(7 * facet_id, ratio) - ratio // 2
    shift_b = jnp.mod(5 * (facet_id // ratio) + 3 * facet_id, ratio) - ratio // 2
    turn = shift_a * jnp.mod(FS * offsets, IMAGE) + shift_b * jnp.mod(FS * column, IMAGE)
    w = unit(turn, IMAGE)
    return cover * w[0], cover * w[1]


def dot(spec, a, b):
    return jnp.einsum(spec, a, b, preferred_element_type=jnp.float32)


def shards(facet_image, coverage, row_offsets, column_offset, piece_owner):
    half = lax.axis_index("half")
    facet_id = lax.axis_index("facet")
    pixels = facet_image[0]
    local_rows = FS // 2
    per_half = SUBGRIDS // 2
    offsets = lax.dynamic_slice_in_dim(row_offsets, half * per_half, per_half, 0)
    cover = lax.dynamic_slice_in_dim(coverage[0], half * per_half, per_half, 0)

    coarse = FINE * jnp.arange(FS // FINE, dtype=jnp.int32) - FS // 2
    col = window(coarse, column_offset)
    col = jnp.concatenate([col[0][0], col[1][0]], axis=1)
    folded = jnp.dot(pixels, col, preferred_element_type=jnp.float32).astype(jnp.bfloat16)
    other = lax.ppermute(folded, "half", [(0, 1), (1, 0)])

    def part_of(which, block):
        first = FINE * jnp.arange(local_rows // FINE, dtype=jnp.int32)
        row = window(first + which * local_rows - FS // 2, offsets)
        row = jnp.concatenate(row, axis=2)
        return dot("sra,rb->sab", row, block)

    blocks = part_of(half, folded) + part_of(1 - half, other)
    part = (
        blocks[:, :M, :M] - blocks[:, M:, M:],
        blocks[:, :M, M:] + blocks[:, M:, :M],
    )
    w = facet_weight(facet_id, offsets, column_offset[0], cover.astype(jnp.float32))
    y = cmul((w[0][:, None, None], w[1][:, None, None]), part)
    y = jnp.stack(y, axis=1).astype(jnp.bfloat16)
    y = y.reshape(per_half, 2, GROUP, KB, M).transpose(2, 0, 1, 3, 4)
    groups = [
        [(x * NZ + z) * NY + v for x in range(NX) for v in range(NY)] for z in range(NZ)
    ]
    y = lax.all_to_all(
        y, "facet", split_axis=0, concat_axis=0, axis_index_groups=groups, tiled=True
    )
    y = jnp.sum(y, axis=0, dtype=jnp.float32).astype(jnp.bfloat16)

    grid = grid_table()
    wide = jnp.concatenate(grid, axis=1)
    full = dot("sckl,lj->sckj", y, wide)
    spread = jnp.stack(
        [
            full[:, 0, :, :SG] - full[:, 1, :, SG:],
            full[:, 0, :, SG:] + full[:, 1, :, :SG],
        ],
        axis=1,
    ).astype(jnp.bfloat16)
    width = 16
    blocks_per = SG // width
    pieces = spread.reshape(per_half, 2, KB, blocks_per, width)
    pieces = pieces.transpose(0, 3, 1, 2, 4).reshape(per_half * blocks_per, 2 * KB * width)

    owners = lax.dynamic_index_in_dim(piece_owner, half, 0, keepdims=False)
    count = owners.shape[0]
    place = jnp.arange(count, dtype=jnp.int32)
    same = (owners[:, None] == owners[None, :]) & (place[:, None] < place[None, :])
    slot_of = jnp.sum(same.astype(jnp.int32), axis=0)
    target = jnp.arange(count * CAP, dtype=jnp.int32)
    pick = (target[:, None] == (owners * CAP + slot_of)[None, :]).astype(jnp.bfloat16)
    outbox = jnp.dot(pick, pieces, preferred_element_type=jnp.float32)
    outbox = outbox.astype(jnp.bfloat16).reshape(count, CAP * 2 * KB * width // 128, 128)
    inbox = lax.all_to_all(outbox, "facet", split_axis=0, concat_axis=0, tiled=True)

    inbox = inbox.reshape(NX, NZ, NY, CAP, 2, KB, width)
    summed = jnp.sum(inbox, axis=1, dtype=jnp.float32) * (1.0 / math.sqrt(count))
    summed = summed.astype(jnp.bfloat16).transpose(2, 3, 5, 0, 1, 4)
    summed = summed.reshape(CAP, 2, width, M)
    out = dot("cdjk,ki->cdji", summed, wide)
    out_re = out[:, 0, :, :SG] - out[:, 1, :, SG:]
    out_im = out[:, 0, :, SG:] + out[:, 1, :, :SG]
    return jnp.stack([out_re, out_im], axis=1)[None, None]


def solution(mesh):
    return jax.shard_map(
        shards,
        mesh=mesh,
        in_specs=(P("facet", "half", None), P("facet", None), P(), P(), P()),
        out_specs=P("half", "facet", None, None, None, None),
        check_vma=False,
    )
```

```python
import functools
import math

import jax
import jax.numpy as jnp
from jax import lax
from jax.experimental import pallas as pl
from jax.experimental.pallas import tpu as pltpu
from jax.sharding import PartitionSpec as P

FS = 2048
M = 256
SG = 512
IMAGE = 131072
SUBGRIDS = 8
CAP = 3
NX, NZ, NY = 4, 8, 4
GROUP = NX * NY
KB = M // GROUP
FINE = 32
SPAN = 512

TWO_PI = 2.0 * math.pi
STRIDE = IMAGE // FS


def unit(product, period):
    quarter = period // 4
    shifted = product + quarter // 2
    turn = jnp.right_shift(shifted, quarter.bit_length() - 1) & 3
    x = ((shifted & (quarter - 1)) - quarter // 2).astype(jnp.float32) * (TWO_PI / period)
    z = x * x
    s = x + x * z * (-1.0 / 6 + z * (1.0 / 120 + z * (-1.0 / 5040 + z * (1.0 / 362880))))
    c = 1.0 + z * (-0.5 + z * (1.0 / 24 + z * (-1.0 / 720 + z * (1.0 / 40320))))
    odd = (turn & 1) == 1
    re = jnp.where(odd, s, c)
    im = jnp.where(odd, c, s)
    return (
        jnp.where((turn == 1) | (turn == 2), -re, re),
        jnp.where(turn >= 2, -im, im),
    )


def cmul(a, b):
    return a[0] * b[0] - a[1] * b[1], a[0] * b[1] + a[1] * b[0]


def taper_of(place):
    relative = place.astype(jnp.float32) * (2.0 / FS)
    return jnp.exp(-2.0 * relative * relative) * (1.0 / math.sqrt(FS))


def fold_kernel(offset_ref, x_hbm, out_ref, big_re, big_im, *scratch):
    steps = FS // SPAN
    images, tables, sem = scratch[:steps], scratch[steps : 2 * steps], scratch[-1]
    copies = [
        pltpu.make_async_copy(x_hbm.at[:, pl.ds(n * SPAN, SPAN)], images[n], sem.at[n])
        for n in range(steps)
    ]
    for copy in copies:
        copy.start()

    def wave(rows, step, start):
        shape = (rows, M)
        place = lax.broadcasted_iota(jnp.int32, shape, 0) * step + start
        tick = (lax.broadcasted_iota(jnp.int32, shape, 1) - M // 2) * STRIDE
        freq = (offset_ref[0] + tick) & (IMAGE - 1)
        return unit(-(place * freq), IMAGE)

    big_re[...], big_im[...] = wave(FS // FINE, FINE, -FS // 2)
    small = wave(FINE, 1, 0)
    row = lax.broadcasted_iota(jnp.int32, (FINE, 128), 0)

    def make(n):
        for m in range(SPAN // FINE):
            at = n * (SPAN // FINE) + m
            big = big_re[at : at + 1, :], big_im[at : at + 1, :]
            taper = taper_of(row + (at * FINE - FS // 2))
            taper = jnp.concatenate([taper, taper], axis=1)
            re, im = cmul(big, small)
            rows = slice(m * FINE, (m + 1) * FINE)
            tables[n][rows, :M] = (taper * re).astype(jnp.bfloat16)
            tables[n][rows, M:] = (taper * im).astype(jnp.bfloat16)

    make(0)
    total = None
    for n in range(steps):
        copies[n].wait()
        if n + 1 < steps:
            make(n + 1)
        term = jnp.dot(
            images[n][...], tables[n][...], preferred_element_type=jnp.float32
        )
        total = term if total is None else total + term
    out_ref[...] = total.astype(jnp.bfloat16)


def fold(pixels, column_offset):
    rows = pixels.shape[0]
    steps = FS // SPAN
    return pl.pallas_call(
        fold_kernel,
        out_shape=jax.ShapeDtypeStruct((rows, 2 * M), jnp.bfloat16),
        in_specs=[
            pl.BlockSpec(memory_space=pltpu.SMEM),
            pl.BlockSpec(memory_space=pl.ANY),
        ],
        out_specs=pl.BlockSpec(memory_space=pltpu.VMEM),
        scratch_shapes=[
            pltpu.VMEM((FS // FINE, M), jnp.float32),
            pltpu.VMEM((FS // FINE, M), jnp.float32),
        ]
        + [pltpu.VMEM((rows, SPAN), jnp.bfloat16)] * steps
        + [pltpu.VMEM((SPAN, 2 * M), jnp.bfloat16)] * steps
        + [pltpu.SemaphoreType.DMA((steps,))],
        cost_estimate=pl.CostEstimate(
            flops=4 * rows * FS * M, bytes_accessed=rows * FS * 2, transcendentals=0
        ),
        compiler_params=pltpu.CompilerParams(vmem_limit_bytes=24 << 20),
        name="fold",
    )(column_offset, pltpu.with_memory_space_constraint(pixels, pltpu.HBM))


def order(n):
    return jnp.where(n < M // 2, n, M // 2 - 1 - n)


def row_kernel(first, *refs):
    half_ref, offset_ref = refs[:2]
    if first:
        f, out_ref, next_re, next_im, wave_re, wave_im, *tables = refs[2:]
    else:
        w_re, w_im, wave_re, wave_im, acc, f, out_ref, *tables = refs[2:]
    count = len(tables) // 2
    rows = f.shape[0]
    start = (half_ref[0] - 1 if first else 0 - half_ref[0]) * rows

    lane = lax.broadcasted_iota(jnp.int32, (8, rows), 1) + start
    taper = taper_of(lane[:1])
    sub = lax.broadcasted_iota(jnp.int32, (8, rows), 0)
    freq = jnp.zeros((8, rows), jnp.int32)
    for n in range(count):
        freq = jnp.where(sub == n, offset_ref[n] - STRIDE // 2, freq)
    gain = unit(-(lane * freq), IMAGE)
    gain = gain[0] * taper, gain[1] * taper

    wide = 128
    if first:
        shape = (M // 2, wide)
        odd = 2 * lax.broadcasted_iota(jnp.int32, shape, 0) + 1
        place = lax.broadcasted_iota(jnp.int32, shape, 1) + start
        blocks = [unit(-(odd * place), 2 * FS)]
        step = unit(-(odd * wide), 2 * FS)
        while len(blocks) < rows // wide:
            blocks += [cmul(block, step) for block in blocks]
            step = cmul(step, step)
        sign = (2 - (odd & 3)) * (2 * half_ref[0] - 1)
        sign = sign.astype(jnp.float32)
        for n, block in enumerate(blocks):
            at = slice(n * wide, (n + 1) * wide)
            wave_re[:, at], wave_im[:, at] = block
            next_re[:, at], next_im[:, at] = -sign * block[1], sign * block[0]

    def make(n):
        re, im = tables[2 * n], tables[2 * n + 1]
        for m in range(rows // wide):
            at = slice(m * wide, (m + 1) * wide)
            g = gain[0][n : n + 1, at], gain[1][n : n + 1, at]
            d = wave_re[:, at], wave_im[:, at]
            rr, ii, ri, ir = g[0] * d[0], g[1] * d[1], g[0] * d[1], g[1] * d[0]
            re[: M // 2, at] = (rr - ii).astype(jnp.bfloat16)
            im[: M // 2, at] = (ri + ir).astype(jnp.bfloat16)
            re[M // 2 :, at] = (rr + ii).astype(jnp.bfloat16)
            im[M // 2 :, at] = (ir - ri).astype(jnp.bfloat16)

    make(0)
    for n in range(count):
        if n + 1 < count:
            make(n + 1)
        by_re, by_im = (
            jnp.dot(t[...], f[...], preferred_element_type=jnp.float32)
            for t in tables[2 * n : 2 * n + 2]
        )
        part = by_re[:, :M] - by_im[:, M:], by_re[:, M:] + by_im[:, :M]
        if first:
            out_ref[n, 0], out_ref[n, 1] = part
        else:
            part = part[0] + acc[n, 0], part[1] + acc[n, 1]
            y = cmul((w_re[n], w_im[n]), part)
            for c in range(2):
                out_ref[:, n, c] = y[c].astype(jnp.bfloat16).reshape(GROUP, KB, M)


def row_product(half, offsets, weight, mine, swap):
    rows = mine.shape[0]
    count = offsets.shape[0]
    smem = pl.BlockSpec(memory_space=pltpu.SMEM)
    vmem = pl.BlockSpec(memory_space=pltpu.VMEM)
    wave = jax.ShapeDtypeStruct((M // 2, rows), jnp.float32)
    tables = [pltpu.VMEM((M, rows), jnp.bfloat16)] * (2 * count)
    cost = pl.CostEstimate(
        flops=8 * count * rows * M * M, bytes_accessed=4 << 20, transcendentals=0
    )
    params = pltpu.CompilerParams(vmem_limit_bytes=24 << 20)
    half = half.reshape(1)
    acc, next_re, next_im = pl.pallas_call(
        functools.partial(row_kernel, True),
        out_shape=(jax.ShapeDtypeStruct((count, 2, M, M), jnp.float32), wave, wave),
        in_specs=[smem, smem, vmem],
        out_specs=(vmem, vmem, vmem),
        scratch_shapes=[pltpu.VMEM(wave.shape, wave.dtype)] * 2 + tables,
        cost_estimate=cost,
        compiler_params=params,
        name="row_mine",
    )(half, offsets, mine)
    other = swap()
    return pl.pallas_call(
        functools.partial(row_kernel, False),
        out_shape=jax.ShapeDtypeStruct((GROUP, count, 2, KB, M), jnp.bfloat16),
        in_specs=[smem] * 4 + [vmem] * 4,
        out_specs=vmem,
        scratch_shapes=tables,
        cost_estimate=cost,
        compiler_params=params,
        name="row_other",
    )(half, offsets, *weight, next_re, next_im, acc, other)


def grid_table(ticks_in):
    ticks_out = jnp.arange(SG, dtype=jnp.int32) - SG // 2
    grid = unit(ticks_in[:, None] * ticks_out[None, :], SG)
    return [(g * (1.0 / math.sqrt(M))).astype(jnp.bfloat16) for g in grid]


def facet_weight(facet_id, offsets, column, cover):
    ratio = STRIDE
    shift_a = (7 * facet_id) % ratio - ratio // 2
    shift_b = (5 * (facet_id // ratio) + 3 * facet_id) % ratio - ratio // 2
    turn = shift_a * ((FS * offsets) & (IMAGE - 1)) + shift_b * ((FS * column) & (IMAGE - 1))
    w = unit(-turn, IMAGE)
    return cover * w[0], cover * w[1]


def dot(spec, a, b):
    return jnp.einsum(spec, a, b, preferred_element_type=jnp.float32)


def shards(facet_image, coverage, row_offsets, column_offset, piece_owner):
    half = lax.axis_index("half")
    facet_id = lax.axis_index("facet")
    per_half = SUBGRIDS // 2
    offsets = lax.dynamic_slice_in_dim(row_offsets, half * per_half, per_half, 0)
    cover = lax.dynamic_slice_in_dim(coverage[0], half * per_half, per_half, 0)

    folded = fold(facet_image[0], column_offset)
    weight = facet_weight(facet_id, offsets, column_offset[0], cover.astype(jnp.float32))
    y = row_product(
        half,
        offsets,
        weight,
        folded,
        lambda: lax.ppermute(folded, "half", [(0, 1), (1, 0)]),
    )
    groups = [
        [(x * NZ + z) * NY + v for x in range(NX) for v in range(NY)] for z in range(NZ)
    ]
    y = lax.all_to_all(
        y, "facet", split_axis=0, concat_axis=0, axis_index_groups=groups, tiled=True
    )
    y = jnp.sum(y, axis=0, dtype=jnp.float32).astype(jnp.bfloat16)

    ticks = jnp.arange(M, dtype=jnp.int32)
    wide = jnp.concatenate(grid_table(ticks - M // 2), axis=1)
    wide_out = jnp.concatenate(grid_table(order(ticks)), axis=1)
    full = dot("sckl,lj->sckj", y, wide)
    spread = jnp.stack(
        [
            full[:, 0, :, :SG] - full[:, 1, :, SG:],
            full[:, 0, :, SG:] + full[:, 1, :, :SG],
        ],
        axis=1,
    ).astype(jnp.bfloat16)
    width = 16
    blocks_per = SG // width
    pieces = spread.reshape(per_half, 2, KB, blocks_per, width)
    pieces = pieces.transpose(0, 3, 1, 2, 4).reshape(per_half * blocks_per, 2 * KB * width)

    owners = lax.dynamic_index_in_dim(piece_owner, half, 0, keepdims=False)
    count = owners.shape[0]
    place = jnp.arange(count, dtype=jnp.int32)
    same = (owners[:, None] == owners[None, :]) & (place[:, None] < place[None, :])
    slot_of = jnp.sum(same.astype(jnp.int32), axis=0)
    target = jnp.arange(count * CAP, dtype=jnp.int32)
    pick = (target[:, None] == (owners * CAP + slot_of)[None, :]).astype(jnp.bfloat16)
    outbox = jnp.dot(pick, pieces, preferred_element_type=jnp.float32)
    outbox = outbox.astype(jnp.bfloat16).reshape(count, CAP, 2 * KB * width // 128, 128)
    inbox = lax.all_to_all(outbox, "facet", split_axis=0, concat_axis=0, tiled=True)

    inbox = inbox.reshape(NX, NZ, NY, CAP, 2 * KB * width // 128, 128)
    summed = jnp.sum(inbox, axis=1, dtype=jnp.float32) * (1.0 / math.sqrt(count))
    summed = lax.optimization_barrier(summed.astype(jnp.bfloat16))
    summed = summed.reshape(NX, NY, CAP, 2, KB, width).transpose(2, 3, 5, 0, 1, 4)
    summed = summed.reshape(CAP, 2, width, M)
    out = dot("cdjk,ki->cdji", summed, wide_out)
    out_re = out[:, 0, :, :SG] - out[:, 1, :, SG:]
    out_im = out[:, 0, :, SG:] + out[:, 1, :, :SG]
    return jnp.stack([out_re, out_im], axis=1)[None, None]


def solution(mesh):
    return jax.shard_map(
        shards,
        mesh=mesh,
        in_specs=(P("facet", "half", None), P("facet", None), P(), P(), P()),
        out_specs=P("half", "facet", None, None, None, None),
        check_vma=False,
    )
```

```python
import functools
import math

import jax
import jax.numpy as jnp
from jax import lax
from jax.experimental import pallas as pl
from jax.experimental.pallas import tpu as pltpu
from jax.sharding import PartitionSpec as P

FS = 2048
M = 256
SG = 512
IMAGE = 131072
SUBGRIDS = 8
CAP = 3
NX, NZ, NY = 4, 8, 4
GROUP = NX * NY
KB = M // GROUP
FINE = 32
SPAN = 512
WIDTH = 16

TWO_PI = 2.0 * math.pi
STRIDE = IMAGE // FS


def unit(product, period):
    quarter = period // 4
    shifted = product + quarter // 2
    turn = jnp.right_shift(shifted, quarter.bit_length() - 1) & 3
    x = ((shifted & (quarter - 1)) - quarter // 2).astype(jnp.float32) * (TWO_PI / period)
    z = x * x
    s = x + x * z * (-1.0 / 6 + z * (1.0 / 120 + z * (-1.0 / 5040 + z * (1.0 / 362880))))
    c = 1.0 + z * (-0.5 + z * (1.0 / 24 + z * (-1.0 / 720 + z * (1.0 / 40320))))
    odd = (turn & 1) == 1
    re = jnp.where(odd, s, c)
    im = jnp.where(odd, c, s)
    return (
        jnp.where((turn == 1) | (turn == 2), -re, re),
        jnp.where(turn >= 2, -im, im),
    )


def cmul(a, b):
    return a[0] * b[0] - a[1] * b[1], a[0] * b[1] + a[1] * b[0]


def taper_of(place):
    relative = place.astype(jnp.float32) * (2.0 / FS)
    return jnp.exp(-2.0 * relative * relative) * (1.0 / math.sqrt(FS))


def fold_kernel(offset_ref, x_hbm, out_ref, big_re, big_im, *scratch):
    steps = FS // SPAN
    images, tables, sem = scratch[:steps], scratch[steps : 2 * steps], scratch[-1]
    copies = [
        pltpu.make_async_copy(x_hbm.at[:, pl.ds(n * SPAN, SPAN)], images[n], sem.at[n])
        for n in range(steps)
    ]
    for copy in copies:
        copy.start()

    def wave(rows, step, start):
        shape = (rows, M)
        place = lax.broadcasted_iota(jnp.int32, shape, 0) * step + start
        tick = (lax.broadcasted_iota(jnp.int32, shape, 1) - M // 2) * STRIDE
        freq = (offset_ref[0] + tick) & (IMAGE - 1)
        return unit(-(place * freq), IMAGE)

    big_re[...], big_im[...] = wave(FS // FINE, FINE, -FS // 2)
    small = wave(FINE, 1, 0)
    row = lax.broadcasted_iota(jnp.int32, (FINE, 128), 0)

    def make(n):
        for m in range(SPAN // FINE):
            at = n * (SPAN // FINE) + m
            big = big_re[at : at + 1, :], big_im[at : at + 1, :]
            taper = taper_of(row + (at * FINE - FS // 2))
            taper = jnp.concatenate([taper, taper], axis=1)
            re, im = cmul(big, small)
            rows = slice(m * FINE, (m + 1) * FINE)
            tables[n][rows, :M] = (taper * re).astype(jnp.bfloat16)
            tables[n][rows, M:] = (taper * im).astype(jnp.bfloat16)

    make(0)
    total = None
    for n in range(steps):
        copies[n].wait()
        if n + 1 < steps:
            make(n + 1)
        term = jnp.dot(
            images[n][...], tables[n][...], preferred_element_type=jnp.float32
        )
        total = term if total is None else total + term
    out_ref[...] = total.astype(jnp.bfloat16)


def fold(pixels, column_offset):
    rows = pixels.shape[0]
    steps = FS // SPAN
    return pl.pallas_call(
        fold_kernel,
        out_shape=jax.ShapeDtypeStruct((rows, 2 * M), jnp.bfloat16),
        in_specs=[
            pl.BlockSpec(memory_space=pltpu.SMEM),
            pl.BlockSpec(memory_space=pl.ANY),
        ],
        out_specs=pl.BlockSpec(memory_space=pltpu.VMEM),
        scratch_shapes=[
            pltpu.VMEM((FS // FINE, M), jnp.float32),
            pltpu.VMEM((FS // FINE, M), jnp.float32),
        ]
        + [pltpu.VMEM((rows, SPAN), jnp.bfloat16)] * steps
        + [pltpu.VMEM((SPAN, 2 * M), jnp.bfloat16)] * steps
        + [pltpu.SemaphoreType.DMA((steps,))],
        cost_estimate=pl.CostEstimate(
            flops=4 * rows * FS * M, bytes_accessed=rows * FS * 2, transcendentals=0
        ),
        compiler_params=pltpu.CompilerParams(vmem_limit_bytes=24 << 20),
        name="fold",
    )(column_offset, pltpu.with_memory_space_constraint(pixels, pltpu.HBM))


def order(n):
    return jnp.where(n < M // 2, n, M // 2 - 1 - n)


def row_kernel(first, *refs):
    half_ref, offset_ref = refs[:2]
    if first:
        f, out_ref, next_re, next_im, wave_re, wave_im, *tables = refs[2:]
    else:
        w_re, w_im, wave_re, wave_im, acc, f, out_ref, zero, box, sem, *tables = refs[2:]
        zero[...] = jnp.zeros_like(zero)
        copies = []
    count = len(tables) // 2
    rows = f.shape[0]
    start = (half_ref[0] - 1 if first else 0 - half_ref[0]) * rows

    lane = lax.broadcasted_iota(jnp.int32, (8, rows), 1) + start
    taper = taper_of(lane[:1])
    sub = lax.broadcasted_iota(jnp.int32, (8, rows), 0)
    freq = jnp.zeros((8, rows), jnp.int32)
    for n in range(count):
        freq = jnp.where(sub == n, offset_ref[n] - STRIDE // 2, freq)
    gain = unit(-(lane * freq), IMAGE)
    gain = gain[0] * taper, gain[1] * taper

    wide = 128
    if first:
        shape = (M // 2, wide)
        odd = 2 * lax.broadcasted_iota(jnp.int32, shape, 0) + 1
        place = lax.broadcasted_iota(jnp.int32, shape, 1) + start
        blocks = [unit(-(odd * place), 2 * FS)]
        step = unit(-(odd * wide), 2 * FS)
        while len(blocks) < rows // wide:
            blocks += [cmul(block, step) for block in blocks]
            step = cmul(step, step)
        sign = (2 - (odd & 3)) * (2 * half_ref[0] - 1)
        sign = sign.astype(jnp.float32)
        for n, block in enumerate(blocks):
            at = slice(n * wide, (n + 1) * wide)
            wave_re[:, at], wave_im[:, at] = block
            next_re[:, at], next_im[:, at] = -sign * block[1], sign * block[0]

    def make(n):
        re, im = tables[2 * n], tables[2 * n + 1]
        for m in range(rows // wide):
            at = slice(m * wide, (m + 1) * wide)
            g = gain[0][n : n + 1, at], gain[1][n : n + 1, at]
            d = wave_re[:, at], wave_im[:, at]
            rr, ii, ri, ir = g[0] * d[0], g[1] * d[1], g[0] * d[1], g[1] * d[0]
            re[: M // 2, at] = (rr - ii).astype(jnp.bfloat16)
            im[: M // 2, at] = (ri + ir).astype(jnp.bfloat16)
            re[M // 2 :, at] = (rr + ii).astype(jnp.bfloat16)
            im[M // 2 :, at] = (ir - ri).astype(jnp.bfloat16)

    make(0)
    for n in range(count):
        if n + 1 < count:
            make(n + 1)
        by_re, by_im = (
            jnp.dot(t[...], f[...], preferred_element_type=jnp.float32)
            for t in tables[2 * n : 2 * n + 2]
        )
        part = by_re[:, :M] - by_im[:, M:], by_re[:, M:] + by_im[:, :M]
        if first:
            out_ref[n, 0], out_ref[n, 1] = part
        else:
            part = part[0] + acc[n, 0], part[1] + acc[n, 1]
            y = cmul((w_re[n], w_im[n]), part)
            for c in range(2):
                box[n, :, c] = y[c].astype(jnp.bfloat16).reshape(GROUP, KB, M)
            copies.append(pltpu.make_async_copy(box.at[n], out_ref.at[:, n], sem.at[n]))
            copies[n].start()
    if not first:
        for copy in copies:
            copy.wait()


def row_product(half, offsets, weight, mine, swap):
    rows = mine.shape[0]
    count = offsets.shape[0]
    smem = pl.BlockSpec(memory_space=pltpu.SMEM)
    vmem = pl.BlockSpec(memory_space=pltpu.VMEM)
    wave = jax.ShapeDtypeStruct((M // 2, rows), jnp.float32)
    tables = [pltpu.VMEM((M, rows), jnp.bfloat16)] * (2 * count)
    cost = pl.CostEstimate(
        flops=8 * count * rows * M * M, bytes_accessed=4 << 20, transcendentals=0
    )
    params = pltpu.CompilerParams(vmem_limit_bytes=24 << 20)
    half = half.reshape(1)
    acc, next_re, next_im = pl.pallas_call(
        functools.partial(row_kernel, True),
        out_shape=(jax.ShapeDtypeStruct((count, 2, M, M), jnp.float32), wave, wave),
        in_specs=[smem, smem, vmem],
        out_specs=(vmem, vmem, vmem),
        scratch_shapes=[pltpu.VMEM(wave.shape, wave.dtype)] * 2 + tables,
        cost_estimate=cost,
        compiler_params=params,
        name="row_mine",
    )(half, offsets, mine)
    other = swap()
    return pl.pallas_call(
        functools.partial(row_kernel, False),
        out_shape=(
            jax.ShapeDtypeStruct((GROUP, count, 2, KB, M), jnp.bfloat16),
            jax.ShapeDtypeStruct((1, 128), jnp.int32),
        ),
        in_specs=[smem] * 4 + [vmem] * 4,
        out_specs=(pl.BlockSpec(memory_space=pltpu.HBM), vmem),
        scratch_shapes=[
            pltpu.VMEM((count, GROUP, 2, KB, M), jnp.bfloat16),
            pltpu.SemaphoreType.DMA((count,)),
        ]
        + tables,
        cost_estimate=cost,
        compiler_params=params,
        name="row_other",
    )(half, offsets, *weight, next_re, next_im, acc, other)


def grid(tick_in, tick_out):
    wave = unit(tick_in * tick_out, SG)
    return [g * (1.0 / math.sqrt(M)) for g in wave]


def spread_table(zero):
    shape = (SG, 2 * M)
    tick_out = lax.broadcasted_iota(jnp.int32, shape, 0) - SG // 2
    spot = lax.broadcasted_iota(jnp.int32, shape, 1) + jnp.tile(zero, (1, shape[1] // 128))
    re, im = grid((spot & (M - 1)) - M // 2, tick_out)
    return jnp.where(spot < M, re, im).astype(jnp.bfloat16)


def finish_table(zero):
    shape = (2 * M, 2 * SG)
    row = lax.broadcasted_iota(jnp.int32, shape, 0)
    spot = lax.broadcasted_iota(jnp.int32, shape, 1) + jnp.tile(zero, (1, shape[1] // 128))
    tick_in = order(row // (2 * KB) * KB + row % KB)
    re, im = grid(tick_in, (spot & (SG - 1)) - SG // 2)
    part = (row // KB) & 1
    same = part == spot // SG
    table = jnp.where(same, re, jnp.where(part == 1, -im, im))
    return table.astype(jnp.bfloat16)


def shuffle(rows, start):
    lane = lax.broadcasted_iota(jnp.int32, rows[0].shape, 1)
    chunk = 128 // len(rows)
    out = None
    for n, row in enumerate(rows):
        shift = (n - start) * chunk % 128
        row = pltpu.roll(row, shift, 1) if shift else row
        out = row if out is None else jnp.where(lane < n * chunk, out, row)
    return out


def spread_kernel(y_ref, grid_ref, pick_ref, out_ref, full, pieces):
    total = y_ref[0].astype(jnp.float32)
    for n in range(1, GROUP):
        total = total + y_ref[n].astype(jnp.float32)
    turned = []
    for n in range(0, total.shape[0], 2 * KB):
        turned += [-total[n + KB : n + 2 * KB], total[n : n + KB]]
    both = jnp.concatenate([total, jnp.concatenate(turned, axis=0)], axis=1)
    full[...] = lax.dot_general(
        grid_ref[...],
        both.astype(jnp.bfloat16),
        (((1,), (1,)), ((), ())),
        preferred_element_type=jnp.float32,
    )
    blocks = SG // WIDTH
    for t in range(WIDTH // 4):
        rows = [full[pl.ds(4 * q + t, blocks, stride=WIDTH), :] for q in range(4)]
        for n in range(4):
            part = shuffle(rows, n).astype(jnp.bfloat16)
            pieces[n * blocks : (n + 1) * blocks, t * 128 : (t + 1) * 128] = part
    out_ref[...] = jnp.dot(
        pick_ref[...], pieces[...], preferred_element_type=jnp.float32
    ).astype(jnp.bfloat16)


def spread(y, table, pick):
    vmem = pl.BlockSpec(memory_space=pltpu.VMEM)
    return pl.pallas_call(
        spread_kernel,
        out_shape=jax.ShapeDtypeStruct((pick.shape[0], 512), jnp.bfloat16),
        in_specs=[vmem] * 3,
        out_specs=vmem,
        scratch_shapes=[
            pltpu.VMEM((SG, 128), jnp.float32),
            pltpu.VMEM((128, 512), jnp.bfloat16),
        ],
        compiler_params=pltpu.CompilerParams(vmem_limit_bytes=16 << 20),
        name="spread",
    )(y.reshape(GROUP, 128, M), table, pick)


def finish_kernel(scale, sum_ref, table_ref, out_ref, rows):
    rows[...] = jnp.zeros_like(rows)
    count = sum_ref.shape[1]
    for q in range(4):
        for g in range(GROUP // 4):
            part = shuffle([sum_ref[4 * g + r] * scale for r in range(4)], q)
            at = slice(g * 128, (g + 1) * 128)
            rows[q * 16 : q * 16 + count, at] = part.astype(jnp.bfloat16)
    out = jnp.dot(rows[...], table_ref[...], preferred_element_type=jnp.float32)
    for q in range(4):
        for c in range(CAP):
            at = q * 16 + c * 4
            for d in range(2):
                out_ref[c, d, 4 * q : 4 * q + 4, :] = out[
                    at : at + 4, d * SG : (d + 1) * SG
                ]


def finish(total, table, scale):
    vmem = pl.BlockSpec(memory_space=pltpu.VMEM)
    return pl.pallas_call(
        functools.partial(finish_kernel, scale),
        out_shape=jax.ShapeDtypeStruct((CAP, 2, WIDTH, SG), jnp.float32),
        in_specs=[vmem] * 2,
        out_specs=vmem,
        scratch_shapes=[pltpu.VMEM((64, 2 * M), jnp.bfloat16)],
        compiler_params=pltpu.CompilerParams(vmem_limit_bytes=16 << 20),
        name="finish",
    )(total, table)


def facet_weight(facet_id, offsets, column, cover):
    ratio = STRIDE
    shift_a = (7 * facet_id) % ratio - ratio // 2
    shift_b = (5 * (facet_id // ratio) + 3 * facet_id) % ratio - ratio // 2
    turn = shift_a * ((FS * offsets) & (IMAGE - 1)) + shift_b * ((FS * column) & (IMAGE - 1))
    w = unit(-turn, IMAGE)
    return cover * w[0], cover * w[1]


def shards(facet_image, coverage, row_offsets, column_offset, piece_owner):
    half = lax.axis_index("half")
    facet_id = lax.axis_index("facet")
    per_half = SUBGRIDS // 2
    offsets = lax.dynamic_slice_in_dim(row_offsets, half * per_half, per_half, 0)
    cover = lax.dynamic_slice_in_dim(coverage[0], half * per_half, per_half, 0)

    folded = fold(facet_image[0], column_offset)
    weight = facet_weight(facet_id, offsets, column_offset[0], cover.astype(jnp.float32))
    y, zero = row_product(
        half,
        offsets,
        weight,
        folded,
        lambda: lax.ppermute(folded, "half", [(0, 1), (1, 0)]),
    )
    groups = [
        [(x * NZ + z) * NY + v for x in range(NX) for v in range(NY)] for z in range(NZ)
    ]
    y = lax.all_to_all(
        y, "facet", split_axis=0, concat_axis=0, axis_index_groups=groups, tiled=True
    )

    owners = lax.dynamic_index_in_dim(piece_owner, half, 0, keepdims=False) + zero[0]
    count = owners.shape[0]
    place = jnp.arange(count, dtype=jnp.int32)
    same = (owners[:, None] == owners[None, :]) & (place[:, None] < place[None, :])
    slot_of = jnp.sum(same.astype(jnp.int32), axis=0)
    target = jnp.arange(count * CAP, dtype=jnp.int32)
    pick = (target[:, None] == (owners * CAP + slot_of)[None, :]).astype(jnp.bfloat16)
    pick, last = lax.optimization_barrier((pick, finish_table(zero)))
    outbox = spread(y, spread_table(zero), pick).reshape(count, CAP, 4, 128)
    inbox = lax.all_to_all(outbox, "facet", split_axis=0, concat_axis=0, tiled=True)

    total = jnp.sum(
        inbox.reshape(NX, NZ, NY, CAP, 4, 128), axis=1, dtype=jnp.float32
    ).reshape(GROUP, CAP * 4, 128)
    return finish(total, last, 1.0 / math.sqrt(count))[None, None]


def solution(mesh):
    return jax.shard_map(
        shards,
        mesh=mesh,
        in_specs=(P("facet", "half", None), P("facet", None), P(), P(), P()),
        out_specs=P("half", "facet", None, None, None, None),
        check_vma=False,
    )
```

```python
import functools
import math

import jax
import jax.numpy as jnp
from jax import lax
from jax.experimental import pallas as pl
from jax.experimental.pallas import tpu as pltpu
from jax.sharding import PartitionSpec as P

FS = 2048
M = 256
SG = 512
IMAGE = 131072
SUBGRIDS = 8
CAP = 3
NX, NZ, NY = 4, 8, 4
PAIR = 2
GROUP = PAIR * NX * NY
KB = M // GROUP
CHUNK = 2 * KB
SLOTS = 128 // CHUNK
FINE = 32
SPAN = 512
WIDTH = 16
ROWS = WIDTH // SLOTS

TWO_PI = 2.0 * math.pi
STRIDE = IMAGE // FS


def unit(product, period):
    quarter = period // 4
    shifted = product + quarter // 2
    turn = jnp.right_shift(shifted, quarter.bit_length() - 1) & 3
    x = ((shifted & (quarter - 1)) - quarter // 2).astype(jnp.float32) * (TWO_PI / period)
    z = x * x
    s = x + x * z * (-1.0 / 6 + z * (1.0 / 120 + z * (-1.0 / 5040 + z * (1.0 / 362880))))
    c = 1.0 + z * (-0.5 + z * (1.0 / 24 + z * (-1.0 / 720 + z * (1.0 / 40320))))
    odd = (turn & 1) == 1
    re = jnp.where(odd, s, c)
    im = jnp.where(odd, c, s)
    return (
        jnp.where((turn == 1) | (turn == 2), -re, re),
        jnp.where(turn >= 2, -im, im),
    )


def cmul(a, b):
    return a[0] * b[0] - a[1] * b[1], a[0] * b[1] + a[1] * b[0]


def taper_of(place):
    relative = place.astype(jnp.float32) * (2.0 / FS)
    return jnp.exp(-2.0 * relative * relative) * (1.0 / math.sqrt(FS))


def fold_kernel(offset_ref, x_hbm, out_ref, big_re, big_im, *scratch):
    steps = FS // SPAN
    images, tables, sem = scratch[:steps], scratch[steps : 2 * steps], scratch[-1]
    copies = [
        pltpu.make_async_copy(x_hbm.at[:, pl.ds(n * SPAN, SPAN)], images[n], sem.at[n])
        for n in range(steps)
    ]
    for copy in copies:
        copy.start()

    def wave(rows, step, start):
        shape = (rows, M)
        place = lax.broadcasted_iota(jnp.int32, shape, 0) * step + start
        tick = (lax.broadcasted_iota(jnp.int32, shape, 1) - M // 2) * STRIDE
        freq = (offset_ref[0] + tick) & (IMAGE - 1)
        return unit(-(place * freq), IMAGE)

    big_re[...], big_im[...] = wave(FS // FINE, FINE, -FS // 2)
    small = wave(FINE, 1, 0)
    row = lax.broadcasted_iota(jnp.int32, (FINE, 128), 0)

    def make(n):
        for m in range(SPAN // FINE):
            at = n * (SPAN // FINE) + m
            big = big_re[at : at + 1, :], big_im[at : at + 1, :]
            taper = taper_of(row + (at * FINE - FS // 2))
            taper = jnp.concatenate([taper, taper], axis=1)
            re, im = cmul(big, small)
            rows = slice(m * FINE, (m + 1) * FINE)
            tables[n][rows, :M] = (taper * re).astype(jnp.bfloat16)
            tables[n][rows, M:] = (taper * im).astype(jnp.bfloat16)

    make(0)
    total = None
    for n in range(steps):
        copies[n].wait()
        if n + 1 < steps:
            make(n + 1)
        term = jnp.dot(
            images[n][...], tables[n][...], preferred_element_type=jnp.float32
        )
        total = term if total is None else total + term
    out_ref[...] = total.astype(jnp.bfloat16)


def fold(pixels, column_offset):
    rows = pixels.shape[0]
    steps = FS // SPAN
    return pl.pallas_call(
        fold_kernel,
        out_shape=jax.ShapeDtypeStruct((rows, 2 * M), jnp.bfloat16),
        in_specs=[
            pl.BlockSpec(memory_space=pltpu.SMEM),
            pl.BlockSpec(memory_space=pl.ANY),
        ],
        out_specs=pl.BlockSpec(memory_space=pltpu.VMEM),
        scratch_shapes=[
            pltpu.VMEM((FS // FINE, M), jnp.float32),
            pltpu.VMEM((FS // FINE, M), jnp.float32),
        ]
        + [pltpu.VMEM((rows, SPAN), jnp.bfloat16)] * steps
        + [pltpu.VMEM((SPAN, 2 * M), jnp.bfloat16)] * steps
        + [pltpu.SemaphoreType.DMA((steps,))],
        cost_estimate=pl.CostEstimate(
            flops=4 * rows * FS * M, bytes_accessed=rows * FS * 2, transcendentals=0
        ),
        compiler_params=pltpu.CompilerParams(vmem_limit_bytes=24 << 20),
        name="fold",
    )(column_offset, pltpu.with_memory_space_constraint(pixels, pltpu.HBM))


def order(n):
    return jnp.where(n < M // 2, n, M // 2 - 1 - n)


def row_kernel(first, *refs):
    half_ref, offset_ref = refs[:2]
    if first:
        f, out_ref, next_re, next_im, wave_re, wave_im, *tables = refs[2:]
    else:
        w_re, w_im, wave_re, wave_im, acc, f, out_ref, zero, box, sem, *tables = refs[2:]
        zero[...] = jnp.zeros_like(zero)
        copies = []
    count = len(tables) // 2
    rows = f.shape[0]
    start = (half_ref[0] - 1 if first else 0 - half_ref[0]) * rows

    lane = lax.broadcasted_iota(jnp.int32, (8, rows), 1) + start
    taper = taper_of(lane[:1])
    sub = lax.broadcasted_iota(jnp.int32, (8, rows), 0)
    freq = jnp.zeros((8, rows), jnp.int32)
    for n in range(count):
        freq = jnp.where(sub == n, offset_ref[n] - STRIDE // 2, freq)
    gain = unit(-(lane * freq), IMAGE)
    gain = gain[0] * taper, gain[1] * taper

    wide = 128
    if first:
        shape = (M // 2, wide)
        odd = 2 * lax.broadcasted_iota(jnp.int32, shape, 0) + 1
        place = lax.broadcasted_iota(jnp.int32, shape, 1) + start
        blocks = [unit(-(odd * place), 2 * FS)]
        step = unit(-(odd * wide), 2 * FS)
        while len(blocks) < rows // wide:
            blocks += [cmul(block, step) for block in blocks]
            step = cmul(step, step)
        sign = (2 - (odd & 3)) * (2 * half_ref[0] - 1)
        sign = sign.astype(jnp.float32)
        for n, block in enumerate(blocks):
            at = slice(n * wide, (n + 1) * wide)
            wave_re[:, at], wave_im[:, at] = block
            next_re[:, at], next_im[:, at] = -sign * block[1], sign * block[0]

    def make(n):
        re, im = tables[2 * n], tables[2 * n + 1]
        for m in range(rows // wide):
            at = slice(m * wide, (m + 1) * wide)
            g = gain[0][n : n + 1, at], gain[1][n : n + 1, at]
            d = wave_re[:, at], wave_im[:, at]
            rr, ii, ri, ir = g[0] * d[0], g[1] * d[1], g[0] * d[1], g[1] * d[0]
            re[: M // 2, at] = (rr - ii).astype(jnp.bfloat16)
            im[: M // 2, at] = (ri + ir).astype(jnp.bfloat16)
            re[M // 2 :, at] = (rr + ii).astype(jnp.bfloat16)
            im[M // 2 :, at] = (ir - ri).astype(jnp.bfloat16)

    make(0)
    for n in range(count):
        if n + 1 < count:
            make(n + 1)
        by_re, by_im = (
            jnp.dot(t[...], f[...], preferred_element_type=jnp.float32)
            for t in tables[2 * n : 2 * n + 2]
        )
        part = by_re[:, :M] - by_im[:, M:], by_re[:, M:] + by_im[:, :M]
        if first:
            out_ref[n, 0], out_ref[n, 1] = part
        else:
            part = part[0] + acc[n, 0], part[1] + acc[n, 1]
            y = cmul((w_re[n], w_im[n]), part)
            y = jnp.concatenate([t.reshape(GROUP, KB, M) for t in y], axis=1)
            box[n] = y.astype(jnp.bfloat16)
            copies.append(pltpu.make_async_copy(box.at[n], out_ref.at[:, n], sem.at[n]))
            copies[n].start()
    if not first:
        for copy in copies:
            copy.wait()


def row_product(half, offsets, weight, mine, swap):
    rows = mine.shape[0]
    count = offsets.shape[0]
    smem = pl.BlockSpec(memory_space=pltpu.SMEM)
    vmem = pl.BlockSpec(memory_space=pltpu.VMEM)
    wave = jax.ShapeDtypeStruct((M // 2, rows), jnp.float32)
    tables = [pltpu.VMEM((M, rows), jnp.bfloat16)] * (2 * count)
    cost = pl.CostEstimate(
        flops=8 * count * rows * M * M, bytes_accessed=4 << 20, transcendentals=0
    )
    params = pltpu.CompilerParams(vmem_limit_bytes=24 << 20)
    half = half.reshape(1)
    acc, next_re, next_im = pl.pallas_call(
        functools.partial(row_kernel, True),
        out_shape=(jax.ShapeDtypeStruct((count, 2, M, M), jnp.float32), wave, wave),
        in_specs=[smem, smem, vmem],
        out_specs=(vmem, vmem, vmem),
        scratch_shapes=[pltpu.VMEM(wave.shape, wave.dtype)] * 2 + tables,
        cost_estimate=cost,
        compiler_params=params,
        name="row_mine",
    )(half, offsets, mine)
    other = swap()
    return pl.pallas_call(
        functools.partial(row_kernel, False),
        out_shape=(
            jax.ShapeDtypeStruct((GROUP, count, CHUNK, M), jnp.bfloat16),
            jax.ShapeDtypeStruct((1, 128), jnp.int32),
        ),
        in_specs=[smem] * 4 + [vmem] * 4,
        out_specs=(pl.BlockSpec(memory_space=pltpu.HBM), vmem),
        scratch_shapes=[
            pltpu.VMEM((count, GROUP, CHUNK, M), jnp.bfloat16),
            pltpu.SemaphoreType.DMA((count,)),
        ]
        + tables,
        cost_estimate=cost,
        compiler_params=params,
        name="row_other",
    )(half, offsets, *weight, next_re, next_im, acc, other)


def grid(tick_in, tick_out):
    wave = unit(tick_in * tick_out, SG)
    return [g * (1.0 / math.sqrt(M)) for g in wave]


def spread_table(zero):
    shape = (SG, 2 * M)
    tick_out = lax.broadcasted_iota(jnp.int32, shape, 0) - SG // 2
    spot = lax.broadcasted_iota(jnp.int32, shape, 1) + jnp.tile(zero, (1, shape[1] // 128))
    re, im = grid((spot & (M - 1)) - M // 2, tick_out)
    return jnp.where(spot < M, re, im).astype(jnp.bfloat16)


def finish_table(zero):
    shape = (2 * M, 2 * SG)
    row = lax.broadcasted_iota(jnp.int32, shape, 0)
    spot = lax.broadcasted_iota(jnp.int32, shape, 1) + jnp.tile(zero, (1, shape[1] // 128))
    x, pair, y = row // (CHUNK * PAIR * NY), row // (CHUNK * NY) % PAIR, row // CHUNK % NY
    tick_in = order(((pair * NX + x) * NY + y) * KB + row % KB)
    re, im = grid(tick_in, (spot & (SG - 1)) - SG // 2)
    part = (row // KB) & 1
    same = part == spot // SG
    table = jnp.where(same, re, jnp.where(part == 1, -im, im))
    return table.astype(jnp.bfloat16)


def shuffle(rows, start):
    lane = lax.broadcasted_iota(jnp.int32, rows[0].shape, 1)
    out = None
    for n, row in enumerate(rows):
        shift = (n - start) * CHUNK % 128
        row = pltpu.roll(row, shift, 1) if shift else row
        out = row if out is None else jnp.where(lane < n * CHUNK, out, row)
    return out


def spread_kernel(y_ref, grid_ref, pick_ref, out_ref, full, pieces):
    total = y_ref[0].astype(jnp.float32)
    for n in range(1, GROUP):
        total = total + y_ref[n].astype(jnp.float32)
    turned = []
    for n in range(0, total.shape[0], CHUNK):
        turned += [-total[n + KB : n + CHUNK], total[n : n + KB]]
    both = jnp.concatenate([total, jnp.concatenate(turned, axis=0)], axis=1)
    count = total.shape[0] // CHUNK
    both = jnp.concatenate([both] * (SLOTS // count), axis=0)
    full[...] = lax.dot_general(
        grid_ref[...],
        both.astype(jnp.bfloat16),
        (((1,), (1,)), ((), ())),
        preferred_element_type=jnp.float32,
    )
    blocks = SG // WIDTH
    for t in range(ROWS):
        rows = [
            full[pl.ds(ROWS * q + t, blocks, stride=WIDTH), :] for q in range(SLOTS)
        ]
        for n in range(count):
            part = shuffle(rows, n).astype(jnp.bfloat16)
            pieces[n * blocks : (n + 1) * blocks, t * 128 : (t + 1) * 128] = part
    out_ref[...] = jnp.dot(
        pick_ref[...], pieces[...], preferred_element_type=jnp.float32
    ).astype(jnp.bfloat16)


def spread(y, table, pick):
    vmem = pl.BlockSpec(memory_space=pltpu.VMEM)
    return pl.pallas_call(
        spread_kernel,
        out_shape=jax.ShapeDtypeStruct((pick.shape[0], ROWS * 128), jnp.bfloat16),
        in_specs=[vmem] * 3,
        out_specs=vmem,
        scratch_shapes=[
            pltpu.VMEM((SG, 128), jnp.float32),
            pltpu.VMEM((pick.shape[1], ROWS * 128), jnp.bfloat16),
        ],
        compiler_params=pltpu.CompilerParams(vmem_limit_bytes=16 << 20),
        name="spread",
    )(y.reshape(GROUP, -1, M), table, pick)


def finish_kernel(scale, sum_ref, table_ref, out_ref, rows):
    rows[...] = jnp.zeros_like(rows)
    count = sum_ref.shape[1]
    for q in range(SLOTS):
        for g in range(GROUP // SLOTS):
            part = [sum_ref[SLOTS * g + r] * scale for r in range(SLOTS)]
            at = slice(g * 128, (g + 1) * 128)
            part = shuffle(part, q).astype(jnp.bfloat16)
            rows[q * 16 : q * 16 + count, at] = part
    out = jnp.dot(rows[...], table_ref[...], preferred_element_type=jnp.float32)
    for q in range(SLOTS):
        for c in range(CAP):
            at = q * 16 + c * ROWS
            for d in range(2):
                out_ref[c, d, ROWS * q : ROWS * (q + 1), :] = out[
                    at : at + ROWS, d * SG : (d + 1) * SG
                ]


def finish(total, table, scale):
    vmem = pl.BlockSpec(memory_space=pltpu.VMEM)
    return pl.pallas_call(
        functools.partial(finish_kernel, scale),
        out_shape=jax.ShapeDtypeStruct((CAP, 2, WIDTH, SG), jnp.float32),
        in_specs=[vmem] * 2,
        out_specs=vmem,
        scratch_shapes=[pltpu.VMEM((16 * SLOTS, 2 * M), jnp.bfloat16)],
        compiler_params=pltpu.CompilerParams(vmem_limit_bytes=16 << 20),
        name="finish",
    )(total, table)


def facet_weight(facet_id, offsets, column, cover):
    ratio = STRIDE
    shift_a = (7 * facet_id) % ratio - ratio // 2
    shift_b = (5 * (facet_id // ratio) + 3 * facet_id) % ratio - ratio // 2
    turn = shift_a * ((FS * offsets) & (IMAGE - 1)) + shift_b * ((FS * column) & (IMAGE - 1))
    w = unit(-turn, IMAGE)
    return cover * w[0], cover * w[1]


def shards(facet_image, coverage, row_offsets, column_offset, piece_owner):
    half = lax.axis_index("half")
    facet_id = lax.axis_index("facet")
    per_half = SUBGRIDS // 2
    offsets = lax.dynamic_slice_in_dim(row_offsets, half * per_half, per_half, 0)
    cover = lax.dynamic_slice_in_dim(coverage[0], half * per_half, per_half, 0)

    folded = fold(facet_image[0], column_offset)
    weight = facet_weight(facet_id, offsets, column_offset[0], cover.astype(jnp.float32))
    y, zero = row_product(
        half,
        offsets,
        weight,
        folded,
        lambda: lax.ppermute(folded, "half", [(0, 1), (1, 0)]),
    )
    groups = [
        [
            (x * NZ + b + z) * NY + v
            for z in range(PAIR)
            for x in range(NX)
            for v in range(NY)
        ]
        for b in range(0, NZ, PAIR)
    ]
    y = lax.all_to_all(
        y, "facet", split_axis=0, concat_axis=0, axis_index_groups=groups, tiled=True
    )

    owners = lax.dynamic_index_in_dim(piece_owner, half, 0, keepdims=False) + zero[0]
    count = owners.shape[0]
    place = jnp.arange(count, dtype=jnp.int32)
    same = (owners[:, None] == owners[None, :]) & (place[:, None] < place[None, :])
    slot_of = jnp.sum(same.astype(jnp.int32), axis=0)
    target = jnp.arange(count * CAP, dtype=jnp.int32)
    pick = (target[:, None] == (owners * CAP + slot_of)[None, :]).astype(jnp.bfloat16)
    pick, last = lax.optimization_barrier((pick, finish_table(zero)))
    outbox = spread(y, spread_table(zero), pick).reshape(count, CAP, ROWS, 128)
    inbox = lax.all_to_all(outbox, "facet", split_axis=0, concat_axis=0, tiled=True)

    total = jnp.sum(
        inbox.reshape(NX, NZ // PAIR, PAIR, NY, CAP, ROWS, 128),
        axis=1,
        dtype=jnp.float32,
    ).reshape(GROUP, CAP * ROWS, 128)
    return finish(total, last, 1.0 / math.sqrt(count))[None, None]


def solution(mesh):
    return jax.shard_map(
        shards,
        mesh=mesh,
        in_specs=(P("facet", "half", None), P("facet", None), P(), P(), P()),
        out_specs=P("half", "facet", None, None, None, None),
        check_vma=False,
    )
```

```python
import functools
import math

import jax
import jax.numpy as jnp
from jax import lax
from jax.experimental import pallas as pl
from jax.experimental.pallas import tpu as pltpu
from jax.sharding import PartitionSpec as P

FS = 2048
M = 256
SG = 512
IMAGE = 131072
SUBGRIDS = 8
CAP = 3
NX, NZ, NY = 4, 8, 4
PAIR = 2
GROUP = PAIR * NX * NY
KB = M // GROUP
CHUNK = 2 * KB
SLOTS = 128 // CHUNK
FINE = 32
SPAN = 256
WIDTH = 16
ROWS = WIDTH // SLOTS

TWO_PI = 2.0 * math.pi
STRIDE = IMAGE // FS


def unit(product, period):
    quarter = period // 4
    shifted = product + quarter // 2
    turn = jnp.right_shift(shifted, quarter.bit_length() - 1) & 3
    x = ((shifted & (quarter - 1)) - quarter // 2).astype(jnp.float32) * (TWO_PI / period)
    z = x * x
    s = x + x * z * (-1.0 / 6 + z * (1.0 / 120 + z * (-1.0 / 5040 + z * (1.0 / 362880))))
    c = 1.0 + z * (-0.5 + z * (1.0 / 24 + z * (-1.0 / 720 + z * (1.0 / 40320))))
    odd = (turn & 1) == 1
    re = jnp.where(odd, s, c)
    im = jnp.where(odd, c, s)
    return (
        jnp.where((turn == 1) | (turn == 2), -re, re),
        jnp.where(turn >= 2, -im, im),
    )


def cmul(a, b):
    return a[0] * b[0] - a[1] * b[1], a[0] * b[1] + a[1] * b[0]


def taper_of(place):
    relative = place.astype(jnp.float32) * (2.0 / FS)
    return jnp.exp(-2.0 * relative * relative) * (1.0 / math.sqrt(FS))


def fold_kernel(offset_ref, x_hbm, out_ref, big_re, big_im, *scratch):
    *images, table, sem = scratch
    copies = [
        pltpu.make_async_copy(x_hbm.at[pl.ds(n * SPAN, SPAN)], image, sem.at[n])
        for n, image in enumerate(images)
    ]
    for copy in copies:
        copy.start()

    def wave(rows, step, start):
        shape = (rows, M)
        place = lax.broadcasted_iota(jnp.int32, shape, 0) * step + start
        tick = (lax.broadcasted_iota(jnp.int32, shape, 1) - M // 2) * STRIDE
        freq = (offset_ref[0] + tick) & (IMAGE - 1)
        return unit(-(place * freq), IMAGE)

    big_re[...], big_im[...] = wave(FS // FINE, FINE, -FS // 2)
    small = wave(FINE, 1, 0)
    row = lax.broadcasted_iota(jnp.int32, (FINE, 128), 0)

    for n in range(FS // FINE):
        big = big_re[n : n + 1, :], big_im[n : n + 1, :]
        taper = taper_of(row + (n * FINE - FS // 2))
        taper = jnp.concatenate([taper, taper], axis=1)
        re, im = cmul(big, small)
        rows = slice(n * FINE, (n + 1) * FINE)
        table[rows, :M] = (taper * re).astype(jnp.bfloat16)
        table[rows, M:] = (taper * im).astype(jnp.bfloat16)
    for n, image in enumerate(images):
        copies[n].wait()
        out_ref[n * SPAN : (n + 1) * SPAN] = jnp.dot(
            image[...], table[...], preferred_element_type=jnp.float32
        ).astype(jnp.bfloat16)


def fold(pixels, column_offset):
    rows = pixels.shape[0]
    steps = rows // SPAN
    return pl.pallas_call(
        fold_kernel,
        out_shape=jax.ShapeDtypeStruct((rows, 2 * M), jnp.bfloat16),
        in_specs=[
            pl.BlockSpec(memory_space=pltpu.SMEM),
            pl.BlockSpec(memory_space=pl.ANY),
        ],
        out_specs=pl.BlockSpec(memory_space=pltpu.VMEM),
        scratch_shapes=[
            pltpu.VMEM((FS // FINE, M), jnp.float32),
            pltpu.VMEM((FS // FINE, M), jnp.float32),
        ]
        + [pltpu.VMEM((SPAN, FS), jnp.bfloat16)] * steps
        + [pltpu.VMEM((FS, 2 * M), jnp.bfloat16)]
        + [pltpu.SemaphoreType.DMA((steps,))],
        cost_estimate=pl.CostEstimate(
            flops=4 * rows * FS * M, bytes_accessed=rows * FS * 2, transcendentals=0
        ),
        compiler_params=pltpu.CompilerParams(vmem_limit_bytes=24 << 20),
        name="fold",
    )(column_offset, pltpu.with_memory_space_constraint(pixels, pltpu.HBM))


def order(n):
    return jnp.where(n < M // 2, n, M // 2 - 1 - n)


def row_kernel(first, *refs):
    half_ref, offset_ref = refs[:2]
    if first:
        f, out_ref, next_re, next_im, wave_re, wave_im, *tables = refs[2:]
    else:
        w_re, w_im, wave_re, wave_im, acc, f, out_ref, zero, box, sem, *tables = refs[2:]
        zero[...] = jnp.zeros_like(zero)
        copies = []
    count = len(tables) // 2
    rows = f.shape[0]
    start = (half_ref[0] - 1 if first else 0 - half_ref[0]) * rows

    lane = lax.broadcasted_iota(jnp.int32, (8, rows), 1) + start
    taper = taper_of(lane[:1])
    sub = lax.broadcasted_iota(jnp.int32, (8, rows), 0)
    freq = jnp.zeros((8, rows), jnp.int32)
    for n in range(count):
        freq = jnp.where(sub == n, offset_ref[n] - STRIDE // 2, freq)
    gain = unit(-(lane * freq), IMAGE)
    gain = gain[0] * taper, gain[1] * taper

    wide = 128
    if first:
        shape = (M // 2, wide)
        odd = 2 * lax.broadcasted_iota(jnp.int32, shape, 0) + 1
        place = lax.broadcasted_iota(jnp.int32, shape, 1) + start
        blocks = [unit(-(odd * place), 2 * FS)]
        step = unit(-(odd * wide), 2 * FS)
        while len(blocks) < rows // wide:
            blocks += [cmul(block, step) for block in blocks]
            step = cmul(step, step)
        sign = (2 - (odd & 3)) * (2 * half_ref[0] - 1)
        sign = sign.astype(jnp.float32)
        for n, block in enumerate(blocks):
            at = slice(n * wide, (n + 1) * wide)
            wave_re[:, at], wave_im[:, at] = block
            next_re[:, at], next_im[:, at] = -sign * block[1], sign * block[0]

    def make(n):
        re, im = tables[2 * n], tables[2 * n + 1]
        for m in range(rows // wide):
            at = slice(m * wide, (m + 1) * wide)
            g = gain[0][n : n + 1, at], gain[1][n : n + 1, at]
            d = wave_re[:, at], wave_im[:, at]
            rr, ii, ri, ir = g[0] * d[0], g[1] * d[1], g[0] * d[1], g[1] * d[0]
            re[: M // 2, at] = (rr - ii).astype(jnp.bfloat16)
            im[: M // 2, at] = (ri + ir).astype(jnp.bfloat16)
            re[M // 2 :, at] = (rr + ii).astype(jnp.bfloat16)
            im[M // 2 :, at] = (ir - ri).astype(jnp.bfloat16)

    make(0)
    for n in range(count):
        if n + 1 < count:
            make(n + 1)
        by_re, by_im = (
            jnp.dot(t[...], f[...], preferred_element_type=jnp.float32)
            for t in tables[2 * n : 2 * n + 2]
        )
        part = by_re[:, :M] - by_im[:, M:], by_re[:, M:] + by_im[:, :M]
        if first:
            out_ref[n, 0], out_ref[n, 1] = part
        else:
            part = part[0] + acc[n, 0], part[1] + acc[n, 1]
            y = cmul((w_re[n], w_im[n]), part)
            y = jnp.concatenate([t.reshape(GROUP, KB, M) for t in y], axis=1)
            box[n] = y.astype(jnp.bfloat16)
            copies.append(pltpu.make_async_copy(box.at[n], out_ref.at[:, n], sem.at[n]))
            copies[n].start()
    if not first:
        for copy in copies:
            copy.wait()


def row_product(half, offsets, weight, mine, swap):
    rows = mine.shape[0]
    count = offsets.shape[0]
    smem = pl.BlockSpec(memory_space=pltpu.SMEM)
    vmem = pl.BlockSpec(memory_space=pltpu.VMEM)
    wave = jax.ShapeDtypeStruct((M // 2, rows), jnp.float32)
    tables = [pltpu.VMEM((M, rows), jnp.bfloat16)] * (2 * count)
    cost = pl.CostEstimate(
        flops=8 * count * rows * M * M, bytes_accessed=4 << 20, transcendentals=0
    )
    params = pltpu.CompilerParams(vmem_limit_bytes=24 << 20)
    half = half.reshape(1)
    acc, next_re, next_im = pl.pallas_call(
        functools.partial(row_kernel, True),
        out_shape=(jax.ShapeDtypeStruct((count, 2, M, M), jnp.float32), wave, wave),
        in_specs=[smem, smem, vmem],
        out_specs=(vmem, vmem, vmem),
        scratch_shapes=[pltpu.VMEM(wave.shape, wave.dtype)] * 2 + tables,
        cost_estimate=cost,
        compiler_params=params,
        name="row_mine",
    )(half, offsets, mine)
    other = swap()
    return pl.pallas_call(
        functools.partial(row_kernel, False),
        out_shape=(
            jax.ShapeDtypeStruct((GROUP, count, CHUNK, M), jnp.bfloat16),
            jax.ShapeDtypeStruct((1, 128), jnp.int32),
        ),
        in_specs=[smem] * 4 + [vmem] * 4,
        out_specs=(pl.BlockSpec(memory_space=pltpu.HBM), vmem),
        scratch_shapes=[
            pltpu.VMEM((count, GROUP, CHUNK, M), jnp.bfloat16),
            pltpu.SemaphoreType.DMA((count,)),
        ]
        + tables,
        cost_estimate=cost,
        compiler_params=params,
        name="row_other",
    )(half, offsets, *weight, next_re, next_im, acc, other)


def grid(tick_in, tick_out):
    wave = unit(tick_in * tick_out, SG)
    return [g * (1.0 / math.sqrt(M)) for g in wave]


def spread_table(zero):
    shape = (SG, 2 * M)
    tick_out = lax.broadcasted_iota(jnp.int32, shape, 0) - SG // 2
    spot = lax.broadcasted_iota(jnp.int32, shape, 1) + jnp.tile(zero, (1, shape[1] // 128))
    re, im = grid((spot & (M - 1)) - M // 2, tick_out)
    return jnp.where(spot < M, re, im).astype(jnp.bfloat16)


def finish_table(zero):
    shape = (2 * M, 2 * SG)
    row = lax.broadcasted_iota(jnp.int32, shape, 0)
    spot = lax.broadcasted_iota(jnp.int32, shape, 1) + jnp.tile(zero, (1, shape[1] // 128))
    x, pair, y = row // (CHUNK * PAIR * NY), row // (CHUNK * NY) % PAIR, row // CHUNK % NY
    tick_in = order(((pair * NX + x) * NY + y) * KB + row % KB)
    re, im = grid(tick_in, (spot & (SG - 1)) - SG // 2)
    part = (row // KB) & 1
    same = part == spot // SG
    table = jnp.where(same, re, jnp.where(part == 1, -im, im))
    return table.astype(jnp.bfloat16)


def shuffle(rows, start):
    lane = lax.broadcasted_iota(jnp.int32, rows[0].shape, 1)
    out = None
    for n, row in enumerate(rows):
        shift = (n - start) * CHUNK % 128
        row = pltpu.roll(row, shift, 1) if shift else row
        out = row if out is None else jnp.where(lane < n * CHUNK, out, row)
    return out


def spread_kernel(y_ref, grid_ref, pick_ref, out_ref, full, pieces):
    total = y_ref[0].astype(jnp.float32)
    for n in range(1, GROUP):
        total = total + y_ref[n].astype(jnp.float32)
    turned = []
    for n in range(0, total.shape[0], CHUNK):
        turned += [-total[n + KB : n + CHUNK], total[n : n + KB]]
    both = jnp.concatenate([total, jnp.concatenate(turned, axis=0)], axis=1)
    count = total.shape[0] // CHUNK
    both = jnp.concatenate([both] * (SLOTS // count), axis=0)
    full[...] = lax.dot_general(
        grid_ref[...],
        both.astype(jnp.bfloat16),
        (((1,), (1,)), ((), ())),
        preferred_element_type=jnp.float32,
    )
    blocks = SG // WIDTH
    for t in range(ROWS):
        rows = [
            full[pl.ds(ROWS * q + t, blocks, stride=WIDTH), :] for q in range(SLOTS)
        ]
        for n in range(count):
            part = shuffle(rows, n).astype(jnp.bfloat16)
            pieces[n * blocks : (n + 1) * blocks, t * 128 : (t + 1) * 128] = part
    out_ref[...] = jnp.dot(
        pick_ref[...], pieces[...], preferred_element_type=jnp.float32
    ).astype(jnp.bfloat16)


def spread(y, table, pick):
    vmem = pl.BlockSpec(memory_space=pltpu.VMEM)
    return pl.pallas_call(
        spread_kernel,
        out_shape=jax.ShapeDtypeStruct((pick.shape[0], ROWS * 128), jnp.bfloat16),
        in_specs=[vmem] * 3,
        out_specs=vmem,
        scratch_shapes=[
            pltpu.VMEM((SG, 128), jnp.float32),
            pltpu.VMEM((pick.shape[1], ROWS * 128), jnp.bfloat16),
        ],
        compiler_params=pltpu.CompilerParams(vmem_limit_bytes=16 << 20),
        name="spread",
    )(y.reshape(GROUP, -1, M), table, pick)


def finish_kernel(scale, sum_ref, table_ref, out_ref, rows):
    rows[...] = jnp.zeros_like(rows)
    count = sum_ref.shape[1]
    for q in range(SLOTS):
        for g in range(GROUP // SLOTS):
            part = [sum_ref[SLOTS * g + r] * scale for r in range(SLOTS)]
            at = slice(g * 128, (g + 1) * 128)
            part = shuffle(part, q).astype(jnp.bfloat16)
            rows[q * 16 : q * 16 + count, at] = part
    out = jnp.dot(rows[...], table_ref[...], preferred_element_type=jnp.float32)
    for q in range(SLOTS):
        for c in range(CAP):
            at = q * 16 + c * ROWS
            for d in range(2):
                out_ref[c, d, ROWS * q : ROWS * (q + 1), :] = out[
                    at : at + ROWS, d * SG : (d + 1) * SG
                ]


def finish(total, table, scale):
    vmem = pl.BlockSpec(memory_space=pltpu.VMEM)
    return pl.pallas_call(
        functools.partial(finish_kernel, scale),
        out_shape=jax.ShapeDtypeStruct((CAP, 2, WIDTH, SG), jnp.float32),
        in_specs=[vmem] * 2,
        out_specs=vmem,
        scratch_shapes=[pltpu.VMEM((16 * SLOTS, 2 * M), jnp.bfloat16)],
        compiler_params=pltpu.CompilerParams(vmem_limit_bytes=16 << 20),
        name="finish",
    )(total, table)


def facet_weight(facet_id, offsets, column, cover):
    ratio = STRIDE
    shift_a = (7 * facet_id) % ratio - ratio // 2
    shift_b = (5 * (facet_id // ratio) + 3 * facet_id) % ratio - ratio // 2
    turn = shift_a * ((FS * offsets) & (IMAGE - 1)) + shift_b * ((FS * column) & (IMAGE - 1))
    w = unit(-turn, IMAGE)
    return cover * w[0], cover * w[1]


def shards(facet_image, coverage, row_offsets, column_offset, piece_owner):
    half = lax.axis_index("half")
    facet_id = lax.axis_index("facet")
    per_half = SUBGRIDS // 2
    offsets = lax.dynamic_slice_in_dim(row_offsets, half * per_half, per_half, 0)
    cover = lax.dynamic_slice_in_dim(coverage[0], half * per_half, per_half, 0)

    folded = fold(facet_image[0], column_offset)
    weight = facet_weight(facet_id, offsets, column_offset[0], cover.astype(jnp.float32))
    y, zero = row_product(
        half,
        offsets,
        weight,
        folded,
        lambda: lax.ppermute(folded, "half", [(0, 1), (1, 0)]),
    )
    groups = [
        [
            (x * NZ + b + z) * NY + v
            for z in range(PAIR)
            for x in range(NX)
            for v in range(NY)
        ]
        for b in range(0, NZ, PAIR)
    ]
    y = lax.all_to_all(
        y, "facet", split_axis=0, concat_axis=0, axis_index_groups=groups, tiled=True
    )

    owners = lax.dynamic_index_in_dim(piece_owner, half, 0, keepdims=False) + zero[0]
    count = owners.shape[0]
    place = jnp.arange(count, dtype=jnp.int32)
    same = (owners[:, None] == owners[None, :]) & (place[:, None] < place[None, :])
    slot_of = jnp.sum(same.astype(jnp.int32), axis=0)
    target = jnp.arange(count * CAP, dtype=jnp.int32)
    pick = (target[:, None] == (owners * CAP + slot_of)[None, :]).astype(jnp.bfloat16)
    pick, last = lax.optimization_barrier((pick, finish_table(zero)))
    outbox = spread(y, spread_table(zero), pick).reshape(count, CAP, ROWS, 128)
    inbox = lax.all_to_all(outbox, "facet", split_axis=0, concat_axis=0, tiled=True)

    total = jnp.sum(
        inbox.reshape(NX, NZ // PAIR, PAIR, NY, CAP, ROWS, 128),
        axis=1,
        dtype=jnp.float32,
    ).reshape(GROUP, CAP * ROWS, 128)
    return finish(total, last, 1.0 / math.sqrt(count))[None, None]


def solution(mesh):
    return jax.shard_map(
        shards,
        mesh=mesh,
        in_specs=(P("facet", "half", None), P("facet", None), P(), P(), P()),
        out_specs=P("half", "facet", None, None, None, None),
        check_vma=False,
    )
```

```python
import functools
import math

import jax
import jax.numpy as jnp
from jax import lax
from jax.experimental import pallas as pl
from jax.experimental.pallas import tpu as pltpu
from jax.sharding import PartitionSpec as P

FS = 2048
M = 256
SG = 512
IMAGE = 131072
SUBGRIDS = 8
CAP = 3
NX, NZ, NY = 4, 8, 4
PAIR = 2
GROUP = PAIR * NX * NY
KB = M // GROUP
CHUNK = 2 * KB
SLOTS = 128 // CHUNK
FINE = 32
SPAN = 256
WIDTH = 16
ROWS = WIDTH // SLOTS

TWO_PI = 2.0 * math.pi
STRIDE = IMAGE // FS


def unit(product, period):
    quarter = period // 4
    shifted = product + quarter // 2
    turn = jnp.right_shift(shifted, quarter.bit_length() - 1) & 3
    x = ((shifted & (quarter - 1)) - quarter // 2).astype(jnp.float32) * (TWO_PI / period)
    z = x * x
    s = x + x * z * (-1.0 / 6 + z * (1.0 / 120 + z * (-1.0 / 5040 + z * (1.0 / 362880))))
    c = 1.0 + z * (-0.5 + z * (1.0 / 24 + z * (-1.0 / 720 + z * (1.0 / 40320))))
    odd = (turn & 1) == 1
    re = jnp.where(odd, s, c)
    im = jnp.where(odd, c, s)
    return (
        jnp.where((turn == 1) | (turn == 2), -re, re),
        jnp.where(turn >= 2, -im, im),
    )


def cmul(a, b):
    return a[0] * b[0] - a[1] * b[1], a[0] * b[1] + a[1] * b[0]


def taper_of(place):
    relative = place.astype(jnp.float32) * (2.0 / FS)
    return jnp.exp(-2.0 * relative * relative) * (1.0 / math.sqrt(FS))


def fold_kernel(offset_ref, x_hbm, out_ref, big_re, big_im, *scratch):
    *images, table, sem = scratch
    copies = [
        pltpu.make_async_copy(x_hbm.at[pl.ds(n * SPAN, SPAN)], image, sem.at[n])
        for n, image in enumerate(images)
    ]
    for copy in copies:
        copy.start()

    def wave(rows, step, start):
        shape = (rows, M)
        place = lax.broadcasted_iota(jnp.int32, shape, 0) * step + start
        tick = (lax.broadcasted_iota(jnp.int32, shape, 1) - M // 2) * STRIDE
        freq = (offset_ref[0] + tick) & (IMAGE - 1)
        return unit(-(place * freq), IMAGE)

    big_re[...], big_im[...] = wave(FS // FINE, FINE, -FS // 2)
    small = wave(FINE, 1, 0)
    row = lax.broadcasted_iota(jnp.int32, (FINE, 128), 0)

    for n in range(FS // FINE):
        big = big_re[n : n + 1, :], big_im[n : n + 1, :]
        taper = taper_of(row + (n * FINE - FS // 2))
        taper = jnp.concatenate([taper, taper], axis=1)
        re, im = cmul(big, small)
        rows = slice(n * FINE, (n + 1) * FINE)
        table[rows, :M] = (taper * re).astype(jnp.bfloat16)
        table[rows, M:] = (taper * im).astype(jnp.bfloat16)
    for n, image in enumerate(images):
        copies[n].wait()
        out_ref[n * SPAN : (n + 1) * SPAN] = jnp.dot(
            image[...], table[...], preferred_element_type=jnp.float32
        ).astype(jnp.bfloat16)


def fold(pixels, column_offset):
    rows = pixels.shape[0]
    steps = rows // SPAN
    return pl.pallas_call(
        fold_kernel,
        out_shape=jax.ShapeDtypeStruct((rows, 2 * M), jnp.bfloat16),
        in_specs=[
            pl.BlockSpec(memory_space=pltpu.SMEM),
            pl.BlockSpec(memory_space=pl.ANY),
        ],
        out_specs=pl.BlockSpec(memory_space=pltpu.VMEM),
        scratch_shapes=[
            pltpu.VMEM((FS // FINE, M), jnp.float32),
            pltpu.VMEM((FS // FINE, M), jnp.float32),
        ]
        + [pltpu.VMEM((SPAN, FS), jnp.bfloat16)] * steps
        + [pltpu.VMEM((FS, 2 * M), jnp.bfloat16)]
        + [pltpu.SemaphoreType.DMA((steps,))],
        cost_estimate=pl.CostEstimate(
            flops=4 * rows * FS * M, bytes_accessed=rows * FS * 2, transcendentals=0
        ),
        compiler_params=pltpu.CompilerParams(vmem_limit_bytes=24 << 20),
        name="fold",
    )(column_offset, pltpu.with_memory_space_constraint(pixels, pltpu.HBM))


def order(n):
    return jnp.where(n < M // 2, n, M // 2 - 1 - n)


def row_kernel(first, *refs):
    half_ref, offset_ref = refs[:2]
    if first:
        f, out_ref, next_re, next_im, wave_re, wave_im, *tables = refs[2:]
    else:
        w_re, w_im, wave_re, wave_im, acc, f, out_ref, zero, box, sem, *tables = refs[2:]
        zero[...] = jnp.zeros_like(zero)
        copies = []
    count = len(tables) // 2
    rows = f.shape[0]
    start = (half_ref[0] - 1 if first else 0 - half_ref[0]) * rows

    lane = lax.broadcasted_iota(jnp.int32, (8, rows), 1) + start
    taper = taper_of(lane[:1])
    sub = lax.broadcasted_iota(jnp.int32, (8, rows), 0)
    freq = jnp.zeros((8, rows), jnp.int32)
    for n in range(count):
        freq = jnp.where(sub == n, offset_ref[n] - STRIDE // 2, freq)
    gain = unit(-(lane * freq), IMAGE)
    gain = gain[0] * taper, gain[1] * taper

    wide = 128
    if first:
        shape = (M // 2, wide)
        odd = 2 * lax.broadcasted_iota(jnp.int32, shape, 0) + 1
        place = lax.broadcasted_iota(jnp.int32, shape, 1) + start
        blocks = [unit(-(odd * place), 2 * FS)]
        step = unit(-(odd * wide), 2 * FS)
        while len(blocks) < rows // wide:
            blocks += [cmul(block, step) for block in blocks]
            step = cmul(step, step)
        sign = (2 - (odd & 3)) * (2 * half_ref[0] - 1)
        sign = sign.astype(jnp.float32)
        for n, block in enumerate(blocks):
            at = slice(n * wide, (n + 1) * wide)
            wave_re[:, at], wave_im[:, at] = block
            next_re[:, at], next_im[:, at] = -sign * block[1], sign * block[0]

    def make(n):
        re, im = tables[2 * n], tables[2 * n + 1]
        for m in range(rows // wide):
            at = slice(m * wide, (m + 1) * wide)
            g = gain[0][n : n + 1, at], gain[1][n : n + 1, at]
            d = wave_re[:, at], wave_im[:, at]
            rr, ii, ri, ir = g[0] * d[0], g[1] * d[1], g[0] * d[1], g[1] * d[0]
            re[: M // 2, at] = (rr - ii).astype(jnp.bfloat16)
            im[: M // 2, at] = (ri + ir).astype(jnp.bfloat16)
            re[M // 2 :, at] = (rr + ii).astype(jnp.bfloat16)
            im[M // 2 :, at] = (ir - ri).astype(jnp.bfloat16)

    make(0)
    for n in range(count):
        if n + 1 < count:
            make(n + 1)
        by_re, by_im = (
            jnp.dot(t[...], f[...], preferred_element_type=jnp.float32)
            for t in tables[2 * n : 2 * n + 2]
        )
        part = by_re[:, :M] - by_im[:, M:], by_re[:, M:] + by_im[:, :M]
        if first:
            out_ref[n, 0], out_ref[n, 1] = part
        else:
            part = part[0] + acc[n, 0], part[1] + acc[n, 1]
            y = cmul((w_re[n], w_im[n]), part)
            y = jnp.concatenate([t.reshape(GROUP, KB, M) for t in y], axis=1)
            box[n] = y.astype(jnp.bfloat16)
            copies.append(pltpu.make_async_copy(box.at[n], out_ref.at[:, n], sem.at[n]))
            copies[n].start()
    if not first:
        for copy in copies:
            copy.wait()


def row_product(half, offsets, weight, mine, swap):
    rows = mine.shape[0]
    count = offsets.shape[0]
    smem = pl.BlockSpec(memory_space=pltpu.SMEM)
    vmem = pl.BlockSpec(memory_space=pltpu.VMEM)
    wave = jax.ShapeDtypeStruct((M // 2, rows), jnp.float32)
    tables = [pltpu.VMEM((M, rows), jnp.bfloat16)] * (2 * count)
    cost = pl.CostEstimate(
        flops=8 * count * rows * M * M, bytes_accessed=4 << 20, transcendentals=0
    )
    params = pltpu.CompilerParams(vmem_limit_bytes=24 << 20)
    half = half.reshape(1)
    acc, next_re, next_im = pl.pallas_call(
        functools.partial(row_kernel, True),
        out_shape=(jax.ShapeDtypeStruct((count, 2, M, M), jnp.float32), wave, wave),
        in_specs=[smem, smem, vmem],
        out_specs=(vmem, vmem, vmem),
        scratch_shapes=[pltpu.VMEM(wave.shape, wave.dtype)] * 2 + tables,
        cost_estimate=cost,
        compiler_params=params,
        name="row_mine",
    )(half, offsets, mine)
    other = swap()
    return pl.pallas_call(
        functools.partial(row_kernel, False),
        out_shape=(
            jax.ShapeDtypeStruct((GROUP, count, CHUNK, M), jnp.bfloat16),
            jax.ShapeDtypeStruct((1, 128), jnp.int32),
        ),
        in_specs=[smem] * 4 + [vmem] * 4,
        out_specs=(pl.BlockSpec(memory_space=pltpu.HBM), vmem),
        scratch_shapes=[
            pltpu.VMEM((count, GROUP, CHUNK, M), jnp.bfloat16),
            pltpu.SemaphoreType.DMA((count,)),
        ]
        + tables,
        cost_estimate=cost,
        compiler_params=params,
        name="row_other",
    )(half, offsets, *weight, next_re, next_im, acc, other)


def grid(tick_in, tick_out):
    wave = unit(tick_in * tick_out, SG)
    return [g * (1.0 / math.sqrt(M)) for g in wave]


def spread_table(zero):
    shape = (SG, 2 * M)
    tick_out = lax.broadcasted_iota(jnp.int32, shape, 0) - SG // 2
    spot = lax.broadcasted_iota(jnp.int32, shape, 1) + jnp.tile(zero, (1, shape[1] // 128))
    re, im = grid((spot & (M - 1)) - M // 2, tick_out)
    return jnp.where(spot < M, re, im).astype(jnp.bfloat16)


def finish_table(zero):
    shape = (2 * M, 2 * SG)
    row = lax.broadcasted_iota(jnp.int32, shape, 0)
    spot = lax.broadcasted_iota(jnp.int32, shape, 1) + jnp.tile(zero, (1, shape[1] // 128))
    x, pair, y = row // (CHUNK * PAIR * NY), row // (CHUNK * NY) % PAIR, row // CHUNK % NY
    tick_in = order(((pair * NX + x) * NY + y) * KB + row % KB)
    re, im = grid(tick_in, (spot & (SG - 1)) - SG // 2)
    part = (row // KB) & 1
    same = part == spot // SG
    table = jnp.where(same, re, jnp.where(part == 1, -im, im))
    return table.astype(jnp.bfloat16)


def shuffle(rows, start):
    lane = lax.broadcasted_iota(jnp.int32, rows[0].shape, 1)
    out = None
    for n, row in enumerate(rows):
        shift = (n - start) * CHUNK % 128
        row = pltpu.roll(row, shift, 1) if shift else row
        out = row if out is None else jnp.where(lane < n * CHUNK, out, row)
    return out


def spread_kernel(y_ref, grid_ref, pick_ref, out_ref, full, pieces):
    total = y_ref[0].astype(jnp.float32)
    for n in range(1, GROUP):
        total = total + y_ref[n].astype(jnp.float32)
    turned = []
    for n in range(0, total.shape[0], CHUNK):
        turned += [-total[n + KB : n + CHUNK], total[n : n + KB]]
    both = jnp.concatenate([total, jnp.concatenate(turned, axis=0)], axis=1)
    count = total.shape[0] // CHUNK
    both = jnp.concatenate([both] * (SLOTS // count), axis=0)
    full[...] = lax.dot_general(
        grid_ref[...],
        both.astype(jnp.bfloat16),
        (((1,), (1,)), ((), ())),
        preferred_element_type=jnp.float32,
    )
    blocks = SG // WIDTH
    for t in range(ROWS):
        rows = [
            full[pl.ds(ROWS * q + t, blocks, stride=WIDTH), :] for q in range(SLOTS)
        ]
        for n in range(count):
            part = shuffle(rows, n).astype(jnp.bfloat16)
            pieces[n * blocks : (n + 1) * blocks, t * 128 : (t + 1) * 128] = part
    out_ref[...] = jnp.dot(
        pick_ref[...], pieces[...], preferred_element_type=jnp.float32
    ).astype(jnp.bfloat16)


def spread(y, table, pick):
    vmem = pl.BlockSpec(memory_space=pltpu.VMEM)
    return pl.pallas_call(
        spread_kernel,
        out_shape=jax.ShapeDtypeStruct((pick.shape[0], ROWS * 128), jnp.bfloat16),
        in_specs=[vmem] * 3,
        out_specs=vmem,
        scratch_shapes=[
            pltpu.VMEM((SG, 128), jnp.float32),
            pltpu.VMEM((pick.shape[1], ROWS * 128), jnp.bfloat16),
        ],
        compiler_params=pltpu.CompilerParams(vmem_limit_bytes=16 << 20),
        name="spread",
    )(y.reshape(GROUP, -1, M), table, pick)


def finish_kernel(scale, sum_ref, table_ref, out_ref, rows):
    rows[...] = jnp.zeros_like(rows)
    count = sum_ref.shape[1]
    for q in range(SLOTS):
        for g in range(GROUP // SLOTS):
            part = [sum_ref[SLOTS * g + r] * scale for r in range(SLOTS)]
            at = slice(g * 128, (g + 1) * 128)
            part = shuffle(part, q).astype(jnp.bfloat16)
            rows[q * 16 : q * 16 + count, at] = part
    out = jnp.dot(rows[...], table_ref[...], preferred_element_type=jnp.float32)
    for q in range(SLOTS):
        for c in range(CAP):
            at = q * 16 + c * ROWS
            for d in range(2):
                out_ref[c, d, ROWS * q : ROWS * (q + 1), :] = out[
                    at : at + ROWS, d * SG : (d + 1) * SG
                ]


def finish(total, table, scale):
    vmem = pl.BlockSpec(memory_space=pltpu.VMEM)
    return pl.pallas_call(
        functools.partial(finish_kernel, scale),
        out_shape=jax.ShapeDtypeStruct((CAP, 2, WIDTH, SG), jnp.float32),
        in_specs=[vmem] * 2,
        out_specs=vmem,
        scratch_shapes=[pltpu.VMEM((16 * SLOTS, 2 * M), jnp.bfloat16)],
        compiler_params=pltpu.CompilerParams(vmem_limit_bytes=16 << 20),
        name="finish",
    )(total, table)


def facet_weight(facet_id, offsets, column, cover):
    ratio = STRIDE
    shift_a = (7 * facet_id) % ratio - ratio // 2
    shift_b = (5 * (facet_id // ratio) + 3 * facet_id) % ratio - ratio // 2
    turn = shift_a * ((FS * offsets) & (IMAGE - 1)) + shift_b * ((FS * column) & (IMAGE - 1))
    w = unit(-turn, IMAGE)
    return cover * w[0], cover * w[1]


def shards(facet_image, coverage, row_offsets, column_offset, piece_owner):
    half = lax.axis_index("half")
    facet_id = lax.axis_index("facet")
    per_half = SUBGRIDS // 2
    offsets = lax.dynamic_slice_in_dim(row_offsets, half * per_half, per_half, 0)
    cover = lax.dynamic_slice_in_dim(coverage[0], half * per_half, per_half, 0)

    folded = fold(facet_image[0], column_offset)
    weight = facet_weight(facet_id, offsets, column_offset[0], cover.astype(jnp.float32))
    y, zero = row_product(
        half,
        offsets,
        weight,
        folded,
        lambda: lax.ppermute(folded, "half", [(0, 1), (1, 0)]),
    )
    groups = [
        [
            (x * NZ + b + z) * NY + v
            for z in range(PAIR)
            for x in range(NX)
            for v in range(NY)
        ]
        for b in range(0, NZ, PAIR)
    ]
    y = lax.all_to_all(
        y, "facet", split_axis=0, concat_axis=0, axis_index_groups=groups, tiled=True
    )

    last = finish_table(zero)
    owners = lax.dynamic_index_in_dim(piece_owner, half, 0, keepdims=False)
    owners = owners + (last[0, :128].astype(jnp.float32) * 0.0).astype(jnp.int32)
    count = owners.shape[0]
    place = jnp.arange(count, dtype=jnp.int32)
    same = (owners[:, None] == owners[None, :]) & (place[:, None] < place[None, :])
    slot_of = jnp.sum(same.astype(jnp.int32), axis=0)
    target = jnp.arange(count * CAP, dtype=jnp.int32)
    pick = (target[:, None] == (owners * CAP + slot_of)[None, :]).astype(jnp.bfloat16)
    pick, last = lax.optimization_barrier((pick, last))
    outbox = spread(y, spread_table(zero), pick).reshape(count, CAP, ROWS, 128)
    inbox = lax.all_to_all(outbox, "facet", split_axis=0, concat_axis=0, tiled=True)

    total = jnp.sum(
        inbox.reshape(NX, NZ // PAIR, PAIR, NY, CAP, ROWS, 128),
        axis=1,
        dtype=jnp.float32,
    ).reshape(GROUP, CAP * ROWS, 128)
    return finish(total, last, 1.0 / math.sqrt(count))[None, None]


def solution(mesh):
    return jax.shard_map(
        shards,
        mesh=mesh,
        in_specs=(P("facet", "half", None), P("facet", None), P(), P(), P()),
        out_specs=P("half", "facet", None, None, None, None),
        check_vma=False,
    )
```
